1024 devices in a mesh: gx: 8 (over y, core), gy: 32 (over z), lev: 4 (over x).
Axes of the slice: x: 4, y: 4, z: 32, core: 2. Of those that a mesh axis runs over, the one named last changes fastest.
Arguments:
- model_state: float32 [2, 16, 2048, 2048], P(None, 'lev', 'gy', 'gx'), as said below
- cutoff: int32 [2, 16], P(None, 'lev'), may hold values from 5 to 10, as said below
- relax_rate: float32 [2, 16], P(None, 'lev'), may hold values from 0.2 to 1
- owner_map: int32 [4, 2], P('lev'), may hold values from 0 to 255
- era_store: float32 [256, 2, 16, 882], P(('gx', 'gy'), None, 'lev'), may hold values from -0.36 to 0.36
Outputs:
- nudged: float32 [2, 16, 2048, 2048], P(None, 'lev', 'gy', 'gx')
The draws below stay inside these ranges and needn't reach their ends.
Inputs may be any that keep to these rules, and one draw needn't show every extreme that they name: `cutoff`: each draw holds both the smallest and the largest value somewhere. `model_state`: finite values of order one.
All inputs are finite; a program needn't handle non-finite values.
Results may differ from the reference program's by a relative error of at most 0.00007.
Values sent between devices are 32-bit elements; how exact they have to be, the bound alone decides.
A program may use at most 32 MiB of HBM per device.

```python
import math
import jax
import jax.numpy as jnp
from jax import lax

NX = 2048
NY = 2048
NVAR = 2
KC = 10
LEV_DEV = 4
NK = 21
LEVELS = 16
N_GX = 8
N_GY = 32
N_LEV = 4


def draw_model_state(key, part):
    subkeys = jax.random.split(key, 6)
    y_pos = jnp.arange(NY, dtype=jnp.int32)[:, None]
    x_pos = jnp.arange(NX, dtype=jnp.int32)[None, :]
    rough = jax.random.normal(subkeys[0], (NVAR, LEVELS, NY, NX), jnp.float32)
    amp_lo, amp_hi = (0.15, 0.45)
    factor = jax.random.uniform(subkeys[1], (NVAR, LEVELS, NY, NX), jnp.float32, 0.5, 1.5)
    total = rough * factor
    wave_x = jax.random.randint(subkeys[2], (6, NVAR, LEVELS, 1, 1), -KC, KC + 1)
    wave_y = jax.random.randint(subkeys[3], (6, NVAR, LEVELS, 1, 1), -KC, KC + 1)
    phases = jax.random.uniform(subkeys[4], (6, NVAR, LEVELS, 1, 1), jnp.float32, 0.0, 6.2831855)
    amplitude = jax.random.uniform(subkeys[5], (6, NVAR, LEVELS, 1, 1), jnp.float32, amp_lo, amp_hi)
    for wave_num in range(6):
        angle_x = jnp.mod(wave_x[wave_num] * x_pos, NX).astype(jnp.float32) * (6.2831855 / NX)
        angle_y = jnp.mod(wave_y[wave_num] * y_pos, NY).astype(jnp.float32) * (6.2831855 / NY)
        total = total + amplitude[wave_num] * jnp.cos(angle_x + angle_y + phases[wave_num])
    return total.astype(jnp.float32)


def draw_cutoff(key, part):
    count = NVAR * LEVELS
    values = jax.random.randint(key, (count,), KC // 2, KC + 1)
    first = jax.random.randint(jax.random.fold_in(key, 1), (), 0, count)
    other = jnp.mod(first + 1 + jax.random.randint(jax.random.fold_in(key, 2), (), 0, count - 1), count)
    values = values.at[first].set(KC)
    values = values.at[other].set(KC // 2)
    return values.reshape(NVAR, LEVELS).astype(jnp.int32)


def with_ends(drawn, stream_key, smallest, top_value):
    index_at = [jax.random.randint(jax.random.fold_in(stream_key, axis), (), 0, length) for axis, length in enumerate(drawn.shape)]
    main_axis = drawn.shape.index(max(drawn.shape))
    neighbour = index_at[:main_axis] + [(index_at[main_axis] + 1) % drawn.shape[main_axis]] + index_at[main_axis + 1:]
    return drawn.at[tuple(index_at)].set(smallest).at[tuple(neighbour)].set(top_value)


def steps_of(own_key, extent, pieces, least, largest):
    factor_of = 1.0
    for dim, blocks in pieces:
        heights = jax.random.uniform(jax.random.fold_in(jax.random.fold_in(own_key, 6), dim), (blocks,), jnp.float32, least / len(pieces), largest / len(pieces))
        factor_of = factor_of * jnp.repeat(jnp.exp(heights), extent[dim] // blocks).reshape((-1,) + (1,) * (len(extent) - 1 - dim))
    return factor_of


def scatter_about(rng, extent, width, reach, cuts=(), kind=jnp.bfloat16):
    entries = width * jax.random.normal(rng, extent, jnp.float32)
    if cuts:
        entries = entries * steps_of(rng, extent, cuts, -0.22, 0.18)
    return jnp.clip(entries, -reach, reach).astype(kind)


def setup_inputs(seed: int = 0) -> dict:
    streams_of = jax.random.split(jax.random.key(seed), 6)
    return {
        "model_state": draw_model_state(jax.random.fold_in(streams_of[5], 71), 0),
        "cutoff": draw_cutoff(jax.random.fold_in(streams_of[5], 71), 0),
        "relax_rate": jnp.clip(jnp.exp(math.log(1.0) - 1.609438 * jax.random.uniform(streams_of[2], (NVAR, LEVELS), jnp.float32) ** steps_of(streams_of[2], (NVAR, LEVELS), ((1, 4),), -0.2, 0.2)), 0.2, 1.0),
        "owner_map": with_ends(jax.random.randint(streams_of[3], (N_LEV, NVAR), 0, N_GX * N_GY), jax.random.fold_in(streams_of[3], 1), 0, (N_GX * N_GY) - 1).astype(jnp.int32),
        "era_store": scatter_about(streams_of[4], (N_GX * N_GY, NVAR, LEVELS, 2 * NK * NK), 0.06, 0.36, ((0, 256), (2, 4)), jnp.float32),
    }


def reference(model_state, cutoff, relax_rate, owner_map, era_store):
    wave_index = jnp.arange(NK, dtype=jnp.int32) - KC
    rows_y = jnp.mod(wave_index, NY)
    cols_x = jnp.mod(wave_index, NX)
    fields = model_state.reshape(NVAR * LEVELS, NY, NX)

    def forward(field):
        full = jnp.fft.fft2(field)
        picked = full[rows_y][:, cols_x] / (NX * NY)
        return jnp.stack([jnp.real(picked), jnp.imag(picked)])

    spectrum = lax.map(forward, fields).reshape(NVAR, LEVELS, 2, NK, NK)
    level_ids = jnp.arange(LEVELS, dtype=jnp.int32)
    owners = owner_map[level_ids // LEV_DEV]
    rows_var = []
    for var_num in range(NVAR):
        rows_var.append(era_store[owners[:, var_num], var_num, level_ids, :])
    analysis = jnp.stack(rows_var).reshape(NVAR, LEVELS, 2, NK, NK)
    total_sq = wave_index[:, None] ** 2 + wave_index[None, :] ** 2
    keep = (total_sq[None, None] <= (cutoff ** 2)[:, :, None, None]).astype(jnp.float32)
    increment = relax_rate[:, :, None, None, None] * keep[:, :, None] * (analysis - spectrum)
    flat_inc = increment.reshape(NVAR * LEVELS, 2, NK, NK)

    def inverse(delta):
        placed = jnp.zeros((NY, NX), dtype=jnp.complex64)
        placed = placed.at[rows_y[:, None], cols_x[None, :]].set(delta[0] + 1j * delta[1])
        return jnp.real(jnp.fft.ifft2(placed)) * (NX * NY)

    added = lax.map(inverse, flat_inc).reshape(NVAR, LEVELS, NY, NX)
    return model_state + added.astype(model_state.dtype)
```

```python
import jax
import jax.numpy as jnp
from jax import lax
from jax.sharding import PartitionSpec as P

NX = 2048
NY = 2048
KC = 10
NK = 21


def tables(positions, length):
    wave_index = jnp.arange(NK, dtype=jnp.int32) - KC
    turns = jnp.mod(positions[:, None] * wave_index[None, :], length).astype(jnp.float32)
    angle = turns * (6.2831855 / length)
    return (jnp.cos(angle), jnp.sin(angle))


def mix(form, left, right):
    return jnp.einsum(form, left, right, precision=lax.Precision.HIGHEST)


def forward_part(field, cos_y, sin_y, cos_x, sin_x):
    along_re = mix("vlyx,yk->vlkx", field, cos_y)
    along_im = -mix("vlyx,yk->vlkx", field, sin_y)
    part_re = mix("vlkx,xj->vlkj", along_re, cos_x) + mix("vlkx,xj->vlkj", along_im, sin_x)
    part_im = mix("vlkx,xj->vlkj", along_im, cos_x) - mix("vlkx,xj->vlkj", along_re, sin_x)
    return jnp.stack([part_re, part_im], axis=2) * (1.0 / (NX * NY))


def inverse_part(increment, cos_y, sin_y, cos_x, sin_x):
    delta_re = increment[:, :, 0]
    delta_im = increment[:, :, 1]
    back_re = mix("vlkj,xj->vlkx", delta_re, cos_x) - mix("vlkj,xj->vlkx", delta_im, sin_x)
    back_im = mix("vlkj,xj->vlkx", delta_re, sin_x) + mix("vlkj,xj->vlkx", delta_im, cos_x)
    return mix("vlkx,yk->vlyx", back_re, cos_y) - mix("vlkx,yk->vlyx", back_im, sin_y)


def body(model_state, cutoff, relax_rate, owner_map, era_store):
    nvar, levels, ny_local, nx_local = model_state.shape
    gx_pos = lax.axis_index("gx")
    gy_pos = lax.axis_index("gy")
    me = gx_pos * lax.axis_size("gy") + gy_pos
    y_pos = gy_pos * ny_local + jnp.arange(ny_local, dtype=jnp.int32)
    x_pos = gx_pos * nx_local + jnp.arange(nx_local, dtype=jnp.int32)
    cos_y, sin_y = tables(y_pos, NY)
    cos_x, sin_x = tables(x_pos, NX)
    mine = (owner_map[0] == me)[:, None, None]
    kept = jnp.where(mine, era_store[0], 0.0).reshape(nvar, levels, 2, NK, NK)
    share = kept - forward_part(model_state, cos_y, sin_y, cos_x, sin_x)
    gap = lax.psum(share, ("gx", "gy"))
    wave_index = jnp.arange(NK, dtype=jnp.int32) - KC
    total_sq = wave_index[:, None] ** 2 + wave_index[None, :] ** 2
    keep = (total_sq[None, None] <= (cutoff**2)[:, :, None, None]).astype(jnp.float32)
    increment = relax_rate[:, :, None, None, None] * keep[:, :, None] * gap
    return model_state + inverse_part(increment, cos_y, sin_y, cos_x, sin_x)


def solution(mesh):
    placed = (
        P(None, "lev", "gy", "gx"),
        P(None, "lev"),
        P(None, "lev"),
        P("lev", None),
        P(("gx", "gy"), None, "lev", None),
    )
    return jax.shard_map(
        body, mesh=mesh, in_specs=placed, out_specs=P(None, "lev", "gy", "gx"), check_vma=False
    )
```

```python
import functools

import jax
import jax.numpy as jnp
import ml_dtypes
import numpy as np
from jax import lax
from jax.experimental import pallas as pl
from jax.experimental.pallas import tpu as pltpu
from jax.sharding import PartitionSpec as P

NX = 2048
NY = 2048
KC = 10
NK = 21
PAD = 24
WIDE = 32
LANES = 512
CHUNKS = LANES // 128
MESH = pl.DeviceIdType.MESH
BF16 = jnp.bfloat16
F32 = jnp.float32


def split(table):
    high = table.astype(ml_dtypes.bfloat16)
    low = (table - high.astype(np.float64)).astype(ml_dtypes.bfloat16)
    return np.stack([high, low])


def wavenumbers():
    return np.concatenate([np.arange(KC + 1), np.arange(1, KC + 1)])


def basis(length):
    wave = wavenumbers()
    angle = 2.0 * np.pi * np.mod(wave[:, None] * np.arange(length)[None, :], length) / length
    is_cos = (np.arange(NK) <= KC)[:, None]
    return np.where(is_cos, np.cos(angle), np.sin(angle))


def along_y_tables(n_gy, fields):
    ny = NY // n_gy
    out = np.zeros((n_gy, PAD, fields * ny))
    out[:, :NK] = np.tile(basis(NY).reshape(NK, n_gy, ny).transpose(1, 0, 2), (1, 1, fields))
    high, low = split(out)
    return np.stack([high, low], axis=1)


def along_x_tables(n_gx):
    nx = NX // n_gx
    out = np.zeros((n_gx, WIDE, nx))
    out[:, :NK] = basis(NX).reshape(NK, n_gx, nx).transpose(1, 0, 2)
    high, low = split(out)
    return np.stack([high, low], axis=1)


def pick_table():
    out = np.zeros((LANES, WIDE))
    p = np.arange(NK * NK)
    out[p, p % NK] = 1.0
    return out.astype(ml_dtypes.bfloat16)


def lane_tables():
    mask = np.zeros((PAD, LANES), np.float32)
    for a in range(NK):
        mask[a, a * NK : (a + 1) * NK] = 1.0
    wave = wavenumbers()
    twice = np.where(wave == 0, 1.0, 2.0)
    rows = np.zeros((16, LANES), np.float32)
    rows[:8, : NK * NK] = (np.outer(twice, twice) / (NX * NY)).reshape(-1)
    rows[8:] = 1e9
    rows[8:, : NK * NK] = (wave[:, None] ** 2 + wave[None, :] ** 2).reshape(-1)
    return mask, rows


def fold_table():
    wave = np.arange(NK) - KC
    number = wavenumbers()
    is_cos = np.arange(NK) <= KC
    hit = (number[:, None] == np.abs(wave)[None, :]).astype(np.float64)
    factor = np.where(is_cos[:, None], hit, hit * np.sign(wave)[None, :])
    both_cos = np.outer(is_cos, is_cos)
    both_sin = np.outer(~is_cos, ~is_cos)
    sign_re = both_cos.astype(np.float64) - both_sin.astype(np.float64)
    sign_im = -(~(both_cos | both_sin)).astype(np.float64)
    out = np.zeros((2, NK, NK, LANES))
    for part, sign in enumerate((sign_re, sign_im)):
        full = np.einsum("ak,bj,ab->kjab", factor, factor, sign)
        out[part, :, :, : NK * NK] = full.reshape(NK, NK, NK * NK)
    return out.reshape(2 * NK * NK, LANES).astype(ml_dtypes.bfloat16)


def halves(value):
    high = value.astype(BF16)
    low = (value - high.astype(F32)).astype(BF16)
    return high, low


def dot(left, right):
    return lax.dot_general(left, right, (((1,), (0,)), ((), ())), preferred_element_type=F32)


def dot_t(left, right):
    return lax.dot_general(left, right, (((1,), (1,)), ((), ())), preferred_element_type=F32)


def blocks(table):
    shape = (4 * PAD, table.shape[2])
    width = table.shape[2] // 4
    row = lax.broadcasted_iota(jnp.int32, shape, 0)
    lane = lax.broadcasted_iota(jnp.int32, shape, 1)
    keep = None
    for f in range(4):
        inside = (row >= f * PAD) & (row < (f + 1) * PAD) & (lane >= f * width) & (lane < (f + 1) * width)
        keep = inside if keep is None else keep | inside
    high, low = table[0].astype(F32), table[1].astype(F32)
    return (
        jnp.where(keep, jnp.concatenate([high] * 4, axis=0), 0.0),
        jnp.where(keep, jnp.concatenate([low] * 4, axis=0), 0.0),
    )


def along_y(block, table):
    high, low = halves(block)
    rows = table.shape[0] // 2
    both = dot(table, high)
    return both[:rows] + both[rows:] + dot(table[:rows], low)


def along_x(value, table, pick, mask):
    high, low = halves(value)
    narrow = dot_t(high, table[0]) + dot_t(high, table[1]) + dot_t(low, table[0])
    high, low = halves(narrow)
    wide = dot_t(high, pick) + dot_t(low, pick)
    return jnp.sum(wide.reshape(8, PAD, LANES) * mask[None], axis=1)


def folded(era, table):
    first = era.astype(BF16).astype(F32)
    rest = era - first
    second = rest.astype(BF16).astype(F32)
    third = rest - second
    out = dot(jnp.concatenate([first, second, third], axis=0).astype(BF16), table)
    return out[:8] + out[8:16] + out[16:24]


def back_x(coefs, table, mask):
    wide = (coefs[:, None, :] * mask[None]).reshape(8 * PAD, LANES)
    high, low = halves(wide)
    return dot(high, table[0]) + dot(high, table[1]) + dot(low, table[0])


def back_y(value, table):
    high, low = halves(value)
    return dot(table[0], high) + dot(table[0], low) + dot(table[1], high)


def kernel(
    n_y, n_z,
    cutoff, relax, owner, state, era, tab_y, tab_x, tab_pick, tab_fold, tab_mask, tab_rows,
    out,
    st, er, ty, tx, pick, fold, mask, rows, by, tx_wide, res, pay, got, got_y, mine_y, total,
    in_sem, out_sem, send_sem, recv_sem,
):
    gx = lax.axis_index("gx")
    gz = lax.axis_index("gy")
    y = gx // 2
    core = gx % 2
    is_root = jnp.logical_and(gz == 0, core == 0)
    is_second = jnp.logical_and(gz == 0, core == 1)
    half_z = n_z // 2

    def at(y_pos, z_pos, core_pos):
        return {"gx": y_pos * 2 + core_pos, "gy": z_pos}

    copies = [
        pltpu.make_async_copy(state.at[0], st.at[pl.ds(0, 4)], in_sem.at[0]),
        pltpu.make_async_copy(state.at[1], st.at[pl.ds(4, 4)], in_sem.at[1]),
        pltpu.make_async_copy(tab_y.at[gz], ty, in_sem.at[2]),
        pltpu.make_async_copy(tab_x.at[gx], tx, in_sem.at[3]),
        pltpu.make_async_copy(tab_mask, mask, in_sem.at[4]),
        pltpu.make_async_copy(era.at[0], er, in_sem.at[5]),
        pltpu.make_async_copy(tab_fold, fold, in_sem.at[6]),
        pltpu.make_async_copy(tab_rows, rows, in_sem.at[7]),
        pltpu.make_async_copy(tab_pick, pick, in_sem.at[8]),
    ]
    for copy in copies:
        copy.start()

    barrier = pltpu.get_barrier_semaphore()

    @pl.when(is_root)
    def _():
        def greet(i, carry):
            pl.semaphore_signal(barrier, inc=1, device_id=at(y, i // 2, i % 2), device_id_type=MESH)
            return carry

        lax.fori_loop(1, 2 * n_z, greet, 0)
        for step in range(1, n_y):
            pl.semaphore_signal(barrier, inc=1, device_id=at((y + step) % n_y, 0, 0), device_id_type=MESH)

    @pl.when(jnp.logical_not(is_root))
    def _():
        far = jnp.logical_and(core == 0, gz >= half_z)
        teller_z = jnp.where(core == 0, 0, gz)
        teller_core = jnp.where(far, 1, 0)
        pl.semaphore_signal(barrier, inc=1, device_id=at(y, teller_z, teller_core), device_id_type=MESH)

    copies[2].wait()
    y_high, y_low = blocks(ty[...])
    y_table = jnp.concatenate([y_high, y_low], axis=0).astype(BF16)
    copies[0].wait()
    low_fields = along_y(st[0:4].reshape(256, 256), y_table)
    copies[1].wait()
    high_fields = along_y(st[4:8].reshape(256, 256), y_table)
    copies[3].wait()
    copies[4].wait()
    copies[8].wait()
    partial = along_x(jnp.concatenate([low_fields, high_fields], axis=0), tx[...], pick[...], mask[...])
    copies[5].wait()
    copies[6].wait()
    held = folded(jnp.concatenate([er[0], er[1]], axis=0), fold[...])
    copies[7].wait()
    row = lax.broadcasted_iota(jnp.int32, (8, LANES), 0)
    me = gx * n_z + gz
    keeper = jnp.where(row < 4, owner[0, 0], owner[0, 1])
    share = jnp.where(keeper == me, held, 0.0) - rows[0:8] * partial
    for c in range(CHUNKS):
        pay[c] = share[:, c * 128 : (c + 1) * 128]

    def prepare():
        for part in range(2):
            tx_wide[part] = dot(pick[...], tx[part]).astype(BF16)
        by[0] = y_high.T.astype(BF16)
        by[1] = y_low.T.astype(BF16)

    rate = jnp.zeros((8, LANES), F32)
    limit = jnp.zeros((8, LANES), jnp.int32)
    for f in range(8):
        rate = jnp.where(row == f, relax[f // 4, f % 4], rate)
        limit = jnp.where(row == f, cutoff[f // 4, f % 4], limit)
    scale = jnp.where(rows[8:16] <= (limit * limit).astype(F32), rate, 0.0)

    def remote(src, dst, which, target):
        return pltpu.make_async_remote_copy(
            src, dst, send_sem.at[which], recv_sem.at[which], device_id=target, device_id_type=MESH
        )

    root = at(y, 0, 0)

    @pl.when(jnp.logical_not(is_root))
    def _():
        waits = jnp.where(is_second, 1 + n_z - half_z, jnp.where(core == 0, 2, 1))
        pl.semaphore_wait(barrier, waits)
        up = remote(pay, got.at[gz * 2 + core - 1], 0, root)
        up.start()
        prepare()
        remote(total, total, 2, root).wait_recv()

        @pl.when(is_second)
        def _():
            def tell(i, carry):
                remote(total, total, 2, at(y, n_z - 1 - i, 0)).start()
                return carry

            lax.fori_loop(0, n_z - half_z, tell, 0)

        @pl.when(jnp.logical_and(core == 0, gz > 0))
        def _():
            remote(total, total, 2, at(y, gz, 1)).start()

    @pl.when(is_root)
    def _():
        pl.semaphore_wait(barrier, half_z + n_y - 1)
        prepare()
        remote(got, got, 0, root).wait_recv()
        mine_y[...] = pay[...] + jnp.sum(got[...], axis=0)
        for step in range(1, n_y):
            remote(mine_y, got_y.at[step - 1], 1, at((y + step) % n_y, 0, 0)).start()
        remote(got_y, got_y, 1, root).wait_recv()
        total[...] = mine_y[...] + jnp.sum(got_y[...], axis=0)
        remote(total, total, 2, at(y, 0, 1)).start()

        def tell(i, carry):
            remote(total, total, 2, at(y, i, 0)).start()
            return carry

        lax.fori_loop(1, half_z, tell, 0)

    summed = jnp.concatenate([total[c] for c in range(CHUNKS)], axis=1)
    middle = back_x(summed * scale, tx_wide[...], mask[...])
    backs = []
    for h in range(2):
        added = back_y(middle[h * 4 * PAD : (h + 1) * 4 * PAD], by[...])
        res[4 * h : 4 * h + 4] = st[4 * h : 4 * h + 4] + added.reshape(4, 64, 256)
        back = pltpu.make_async_copy(res.at[pl.ds(4 * h, 4)], out.at[h], out_sem.at[h])
        back.start()
        backs.append(back)

    @pl.when(is_root)
    def _():
        remote(got_y, got_y, 1, root).wait_send()
        sent = got.at[pl.ds(0, half_z)]
        remote(sent, sent, 2, root).wait_send()

    @pl.when(jnp.logical_not(is_root))
    def _():
        remote(pay, pay, 0, root).wait_send()

    @pl.when(is_second)
    def _():
        sent = got.at[pl.ds(0, n_z - half_z)]
        remote(sent, sent, 2, root).wait_send()

    @pl.when(jnp.logical_and(core == 0, gz > 0))
    def _():
        remote(total, total, 2, root).wait_send()

    for back in backs:
        back.wait()


def solution(mesh):
    n_gx, n_gy = mesh.shape["gx"], mesh.shape["gy"]
    tables = (along_y_tables(n_gy, 4), along_x_tables(n_gx), pick_table(), fold_table(), *lane_tables())

    def body(model_state, cutoff, relax_rate, owner_map, era_store):
        smem = pl.BlockSpec(memory_space=pltpu.SMEM)
        anyw = pl.BlockSpec(memory_space=pl.ANY)
        vmem = pltpu.VMEM
        return pl.pallas_call(
            functools.partial(kernel, n_gx // 2, n_gy),
            out_shape=jax.ShapeDtypeStruct(model_state.shape, F32),
            in_specs=[smem] * 3 + [anyw] * 8,
            out_specs=anyw,
            scratch_shapes=[
                vmem((8, 64, 256), F32),
                vmem((2, 4, 2 * NK * NK), F32),
                vmem((2, PAD, 256), BF16),
                vmem((2, WIDE, 256), BF16),
                vmem((LANES, WIDE), BF16),
                vmem((2 * NK * NK, LANES), BF16),
                vmem((PAD, LANES), F32),
                vmem((16, LANES), F32),
                vmem((2, 256, 4 * PAD), BF16),
                vmem((2, LANES, 256), BF16),
                vmem((8, 64, 256), F32),
                vmem((CHUNKS, 8, 128), F32),
                vmem((2 * n_gy - 1, CHUNKS, 8, 128), F32),
                vmem((n_gx // 2 - 1, CHUNKS, 8, 128), F32),
                vmem((CHUNKS, 8, 128), F32),
                vmem((CHUNKS, 8, 128), F32),
                pltpu.SemaphoreType.DMA((9,)),
                pltpu.SemaphoreType.DMA((2,)),
                pltpu.SemaphoreType.DMA((3,)),
                pltpu.SemaphoreType.DMA((3,)),
            ],
            compiler_params=pltpu.CompilerParams(collective_id=0, has_side_effects=True),
        )(cutoff, relax_rate, owner_map, model_state, era_store, *(jnp.asarray(t) for t in tables))

    placed = (
        P(None, "lev", "gy", "gx"),
        P(None, "lev"),
        P(None, "lev"),
        P("lev", None),
        P(("gx", "gy"), None, "lev", None),
    )
    return jax.shard_map(
        body, mesh=mesh, in_specs=placed, out_specs=P(None, "lev", "gy", "gx"), check_vma=False
    )
```

```python
import functools

import jax
import jax.numpy as jnp
import ml_dtypes
import numpy as np
from jax import lax
from jax.experimental import pallas as pl
from jax.experimental.pallas import tpu as pltpu
from jax.sharding import PartitionSpec as P

NX = 2048
NY = 2048
KC = 10
NK = 21
PAD = 24
WIDE = 32
FIELDS = 8
ROWS = NK * FIELDS
LANES = 512
CHUNKS = LANES // 128
FAR = (12, 20)
MESH = pl.DeviceIdType.MESH
BF16 = jnp.bfloat16
F32 = jnp.float32


def split(table):
    high = table.astype(ml_dtypes.bfloat16)
    low = (table - high.astype(np.float64)).astype(ml_dtypes.bfloat16)
    return np.stack([high, low])


def wavenumbers():
    return np.concatenate([np.arange(KC + 1), np.arange(1, KC + 1)])


def basis(length):
    wave = wavenumbers()
    angle = 2.0 * np.pi * np.mod(wave[:, None] * np.arange(length)[None, :], length) / length
    is_cos = (np.arange(NK) <= KC)[:, None]
    return np.where(is_cos, np.cos(angle), np.sin(angle))


def along_y_tables(n_gy, fields):
    ny = NY // n_gy
    out = np.zeros((n_gy, PAD, fields * ny))
    out[:, :NK] = np.tile(basis(NY).reshape(NK, n_gy, ny).transpose(1, 0, 2), (1, 1, fields))
    high, low = split(out)
    return np.stack([high, low], axis=1)


def along_x_tables(n_gx):
    nx = NX // n_gx
    out = np.zeros((n_gx, WIDE, nx))
    out[:, :NK] = basis(NX).reshape(NK, n_gx, nx).transpose(1, 0, 2)
    high, low = split(out)
    return np.stack([high, low], axis=1)


def pick_table():
    out = np.zeros((LANES, WIDE))
    p = np.arange(NK * NK)
    out[p, p % NK] = 1.0
    return out.astype(ml_dtypes.bfloat16)


def fold_tables():
    wave = np.arange(NK) - KC
    number = wavenumbers()
    is_cos = np.arange(NK) <= KC
    hit = (number[:, None] == np.abs(wave)[None, :]).astype(np.float64)
    factor = np.where(is_cos[:, None], hit, hit * np.sign(wave)[None, :])
    table = np.zeros((NK * NK, LANES))
    table[:, : NK * NK] = np.einsum("ak,bj->kjab", factor, factor).reshape(NK * NK, NK * NK)
    both_cos = np.outer(is_cos, is_cos)
    both_sin = np.outer(~is_cos, ~is_cos)
    twice = np.where(number == 0, 1.0, 2.0)
    kinds = [
        np.outer(twice, twice) / (NX * NY),
        number[:, None] ** 2 + number[None, :] ** 2,
        both_cos.astype(np.float64) - both_sin.astype(np.float64),
        -(~(both_cos | both_sin)).astype(np.float64),
    ]
    rows = np.zeros((4, FIELDS, LANES), np.float32)
    for kind, value in enumerate(kinds):
        rows[kind, :, : NK * NK] = value.reshape(-1)
    return table.astype(ml_dtypes.bfloat16), rows.reshape(4 * FIELDS, LANES)


def halves(value):
    high = value.astype(BF16)
    low = (value - high.astype(F32)).astype(BF16)
    return high, low


def dot(left, right):
    return lax.dot_general(left, right, (((1,), (0,)), ((), ())), preferred_element_type=F32)


def dot_t(left, right):
    return lax.dot_general(left, right, (((1,), (1,)), ((), ())), preferred_element_type=F32)


def blocks(table):
    shape = (FIELDS, 2 * table.shape[2])
    field = lax.broadcasted_iota(jnp.int32, shape, 0)
    lane = lax.broadcasted_iota(jnp.int32, shape, 1)
    width = shape[1] // FIELDS
    keep = (lane >= field * width) & (lane < (field + 1) * width)
    out = []
    for part in range(2):
        half = table[part].astype(F32)
        whole = jnp.concatenate([half, half], axis=1)[:NK]
        out.append(jnp.where(keep[None], whole[:, None, :], 0.0).reshape(ROWS, shape[1]))
    return out


def along_y(block, both_tables, high_table):
    high, low = halves(block)
    both = dot(both_tables, high)
    return both[:ROWS] + both[ROWS:] + dot(high_table, low)


def spans(a):
    return [
        (t, max(a * NK - 128 * t, 0), min((a + 1) * NK - 128 * t, 128))
        for t in range(a * NK // 128, (a * NK + NK - 1) // 128 + 1)
    ]


def along_x(value, table, pick):
    high, low = halves(value)
    narrow = dot_t(high, table[0]) + dot_t(high, table[1]) + dot_t(low, table[0])
    high, low = halves(narrow)
    wide = dot_t(high, pick) + dot_t(low, pick)
    lane = lax.broadcasted_iota(jnp.int32, (FIELDS, 128), 1)
    tiles = [None] * CHUNKS
    for a in range(NK):
        for t, start, _ in spans(a):
            here = wide[a * FIELDS : (a + 1) * FIELDS, t * 128 : (t + 1) * 128]
            tiles[t] = here if tiles[t] is None else jnp.where(lane >= start, here, tiles[t])
    return jnp.concatenate(tiles, axis=1)


def folded(era, table, sign_re, sign_im):
    parts = []
    for part in range(2):
        value = era[:, part * NK * NK : (part + 1) * NK * NK]
        first = value.astype(BF16).astype(F32)
        rest = value - first
        second = rest.astype(BF16).astype(F32)
        parts += [first, second, rest - second]
    out = dot(jnp.concatenate(parts, axis=0).astype(BF16), table)
    real = out[0:8] + out[8:16] + out[16:24]
    imag = out[24:32] + out[32:40] + out[40:48]
    return sign_re * real + sign_im * imag


def spread(coefs):
    lane = lax.broadcasted_iota(jnp.int32, (FIELDS, 128), 1)
    zero = jnp.zeros((FIELDS, 128), F32)
    rows = []
    for a in range(NK):
        tiles = [zero] * CHUNKS
        for t, start, stop in spans(a):
            tiles[t] = jnp.where((lane >= start) & (lane < stop), coefs[:, t * 128 : (t + 1) * 128], 0.0)
        rows.append(jnp.concatenate(tiles, axis=1))
    return jnp.concatenate(rows, axis=0)


def back_x(coefs, table):
    first = coefs.astype(BF16).astype(F32)
    high = spread(first)
    both = dot(jnp.concatenate([high, spread(coefs - first)], axis=0).astype(BF16), table[0])
    return both[:ROWS] + both[ROWS:] + dot(high.astype(BF16), table[1])


def back_y_tables(high, low):
    fill = jnp.zeros((512 - 3 * ROWS, high.shape[1]), F32)
    return jnp.concatenate([high, low, high, fill], axis=0).T.astype(BF16)


def back_y(value, table):
    high = value.astype(BF16).astype(F32)
    fill = jnp.zeros((512 - 3 * ROWS, value.shape[1]), F32)
    return dot(table, jnp.concatenate([high, high, value - high, fill], axis=0).astype(BF16))


def way_back():
    children = {
        (0, 0): [(0, 1), (1, 1), (4, 0), (1, 0), (3, 0), (2, 1), (2, 0), (8, 0)],
        (0, 1): [(31, 0)],
        (4, 0): [(5, 0), (5, 1), (6, 0), (7, 0), (6, 1), (4, 1)],
        (8, 0): [(8, 1), (12, 0), (9, 0), (10, 0), (11, 0)],
        (12, 0): [(12, 1), (13, 0), (14, 0), (15, 0)],
        (19, 0): [(19, 1), (16, 0), (17, 0), (18, 0)],
        (23, 0): [(23, 1), (20, 0), (21, 0), (22, 0)],
        (31, 0): [(31, 1), (19, 0), (23, 0)] + [(z, 0) for z in range(24, 31)],
    }
    parent = {child: node for node, nodes in children.items() for child in nodes}
    for z in range(1, 32):
        if (z, 1) not in parent:
            parent[z, 1] = (z, 0)
            children[z, 0] = [(z, 1)]
    return children, parent


def kernel(
    n_y, n_z,
    cutoff_in, relax_in, owner_in, state, era, tab_y, tab_x, tab_pick, tab_fold, tab_rows,
    out,
    cutoff, relax, owner, st, er, ty, tx, pick, fold, rows, by, tx_wide, scale, pay, got, got_y, mine_y, total,
    in_sem, send_sem, recv_sem,
):
    gx = lax.axis_index("gx")
    gz = lax.axis_index("gy")
    lev = lax.axis_index("lev")
    y = gx // 2
    children, parent = way_back()

    def swapped(y_pos):
        return jnp.where(jnp.logical_and(y_pos == 0, lev == 0), 1, 0)

    def at(y_pos, z_pos, slot):
        flip = swapped(y_pos)
        other = slot + flip - 2 * slot * flip
        return {"gx": y_pos * 2 + jnp.where(z_pos == 0, other, slot), "gy": z_pos}

    flip = swapped(y)
    core = gx % 2
    slot = jnp.where(gz == 0, core + flip - 2 * core * flip, core)
    index = 2 * gz + slot
    is_root = index == 0

    def by_index(table, default):
        value = jnp.int32(default)
        for key, entry in table.items():
            if entry != default:
                value = jnp.where(index == 2 * key[0] + key[1], entry, value)
        return value

    copies = [
        pltpu.make_async_copy(tab_y.at[gz], ty, in_sem.at[0]),
        pltpu.make_async_copy(state.at[0], st.at[pl.ds(0, 4)], in_sem.at[1]),
        pltpu.make_async_copy(state.at[1], st.at[pl.ds(4, 4)], in_sem.at[2]),
        pltpu.make_async_copy(tab_x.at[gx], tx, in_sem.at[3]),
        pltpu.make_async_copy(tab_pick, pick, in_sem.at[4]),
        pltpu.make_async_copy(era.at[0], er, in_sem.at[5]),
        pltpu.make_async_copy(tab_fold, fold, in_sem.at[6]),
        pltpu.make_async_copy(tab_rows, rows, in_sem.at[7]),
        pltpu.make_async_copy(owner_in, owner, in_sem.at[8]),
        pltpu.make_async_copy(cutoff_in, cutoff, in_sem.at[9]),
        pltpu.make_async_copy(relax_in, relax, in_sem.at[10]),
    ]
    for copy in copies:
        copy.start()

    barrier = pltpu.get_barrier_semaphore()

    @pl.when(is_root)
    def _():
        def greet(i, carry):
            pl.semaphore_signal(barrier, inc=1, device_id=at(y, i // 2, i % 2), device_id_type=MESH)
            return carry

        lax.fori_loop(1, 2 * n_z, greet, 0)
        for step in range(1, n_y):
            pl.semaphore_signal(barrier, inc=1, device_id=at((y + step) % n_y, 0, 0), device_id_type=MESH)

    @pl.when(jnp.logical_not(is_root))
    def _():
        parent_z = by_index({key: node[0] for key, node in parent.items() if node[0] != key[0]}, -1)
        parent_z = jnp.where(parent_z < 0, gz, parent_z)
        parent_slot = by_index({key: node[1] for key, node in parent.items()}, 0)
        pl.semaphore_signal(barrier, inc=1, device_id=at(y, parent_z, parent_slot), device_id_type=MESH)

    copies[0].wait()
    y_high, y_low = blocks(ty[...])
    y_both = jnp.concatenate([y_high, y_low], axis=0).astype(BF16)
    copies[1].wait()
    copies[2].wait()
    along = along_y(st[...].reshape(512, 256), y_both, y_high.astype(BF16))
    copies[3].wait()
    copies[4].wait()
    partial = along_x(along, tx[...], pick[...])
    for copy in copies[5:]:
        copy.wait()
    held = folded(jnp.concatenate([er[0], er[1]], axis=0), fold[...], rows[16:24], rows[24:32])
    row = lax.broadcasted_iota(jnp.int32, (8, LANES), 0)
    me = gx * n_z + gz
    keeper = jnp.where(row < 4, owner[0, 0], owner[0, 1])
    share = jnp.where(keeper == me, held, 0.0) - rows[0:8] * partial
    for c in range(CHUNKS):
        pay[c] = share[:, c * 128 : (c + 1) * 128]

    def prepare():
        rate = jnp.zeros((8, LANES), F32)
        limit = jnp.zeros((8, LANES), jnp.int32)
        for f in range(8):
            rate = jnp.where(row == f, relax[f // 4, f % 4], rate)
            limit = jnp.where(row == f, cutoff[f // 4, f % 4], limit)
        scale[...] = jnp.where(rows[8:16] <= (limit * limit).astype(F32), rate, 0.0)
        for part in range(2):
            tx_wide[part] = dot(pick[...], tx[part]).astype(BF16)
        by[...] = back_y_tables(y_high, y_low)

    n_far = 2 * (FAR[1] - FAR[0])
    n_near = 2 * n_z - 1 - n_far

    def remote(src, dst, which, target):
        return pltpu.make_async_remote_copy(
            src, dst, send_sem.at[which % 3], recv_sem.at[which], device_id=target, device_id_type=MESH
        )

    root = at(y, 0, 0)
    busy = [key for key, nodes in children.items() if key == (0, 1) or len(nodes) > 1]
    is_relay = jnp.logical_and(slot == 0, by_index({key: len(nodes) for key, nodes in children.items()}, 0) == 1)

    def pass_on(key):
        for z, child_slot in children[key]:
            remote(total, total, 2, at(y, z, child_slot)).start()

    @pl.when(jnp.logical_not(is_root))
    def _():
        pl.semaphore_wait(barrier, 1 + by_index({key: len(nodes) for key, nodes in children.items()}, 0))
        far = jnp.logical_and(gz >= FAR[0], gz < FAR[1])
        after = jnp.where(gz >= FAR[1], index - 2 * (FAR[1] - FAR[0]), index)
        place = jnp.where(far, n_near + index - 2 * FAR[0], after - 1)
        pltpu.make_async_remote_copy(
            pay, got.at[place], send_sem.at[0], recv_sem.at[jnp.where(far, 3, 0)],
            device_id=root, device_id_type=MESH,
        ).start()
        prepare()
        remote(total, total, 2, root).wait_recv()

    for key in busy:
        if key != (0, 0):
            pl.when(index == 2 * key[0] + key[1])(functools.partial(pass_on, key))

    @pl.when(is_relay)
    def _():
        remote(total, total, 2, at(y, gz, 1)).start()

    @pl.when(is_root)
    def _():
        pl.semaphore_wait(barrier, len(children[0, 0]) + n_y - 1)
        prepare()
        near, far = got.at[pl.ds(0, n_near)], got.at[pl.ds(n_near, n_far)]
        remote(near, near, 0, root).wait_recv()
        first = pay[...] + jnp.sum(near[...], axis=0)
        remote(far, far, 3, root).wait_recv()
        mine_y[...] = first + jnp.sum(far[...], axis=0)
        for step in range(1, n_y):
            remote(mine_y, got_y.at[step - 1], 1, at((y + step) % n_y, 0, 0)).start()
        remote(got_y, got_y, 1, root).wait_recv()
        total[...] = mine_y[...] + jnp.sum(got_y[...], axis=0)
        pass_on((0, 0))

    summed = jnp.concatenate([total[c] for c in range(CHUNKS)], axis=1)
    added = back_y(back_x(summed * scale[...], tx_wide[...]), by[...])
    for h in range(2):
        block = added[256 * h : 256 * (h + 1)].reshape(4, 64, 256)
        out[h] = st[4 * h : 4 * h + 4] + block

    def pass_on_sent(count):
        sent = got.at[pl.ds(0, count)]
        remote(sent, sent, 2, root).wait_send()

    @pl.when(is_root)
    def _():
        remote(got_y, got_y, 1, root).wait_send()

    @pl.when(jnp.logical_not(is_root))
    def _():
        remote(pay, pay, 0, root).wait_send()

    for key in busy:
        pl.when(index == 2 * key[0] + key[1])(functools.partial(pass_on_sent, len(children[key])))

    @pl.when(is_relay)
    def _():
        pass_on_sent(1)


def solution(mesh):
    n_gx, n_gy = mesh.shape["gx"], mesh.shape["gy"]
    tables = (along_y_tables(n_gy, FIELDS // 2), along_x_tables(n_gx), pick_table(), *fold_tables())

    def body(model_state, cutoff, relax_rate, owner_map, era_store):
        arrays = (cutoff, relax_rate, owner_map, model_state, era_store, *(jnp.asarray(t) for t in tables))
        vmem = pltpu.VMEM
        return pl.pallas_call(
            functools.partial(kernel, n_gx // 2, n_gy),
            out_shape=jax.ShapeDtypeStruct(model_state.shape, F32),
            in_specs=[pl.BlockSpec(memory_space=pltpu.HBM)] * 10,
            out_specs=pl.BlockSpec(memory_space=vmem),
            scratch_shapes=[
                pltpu.SMEM((2, 4), jnp.int32),
                pltpu.SMEM((2, 4), F32),
                pltpu.SMEM((1, 2), jnp.int32),
                vmem((8, 64, 256), F32),
                vmem((2, 4, 2 * NK * NK), F32),
                vmem((2, PAD, 256), BF16),
                vmem((2, WIDE, 256), BF16),
                vmem((LANES, WIDE), BF16),
                vmem((NK * NK, LANES), BF16),
                vmem((4 * FIELDS, LANES), F32),
                vmem((512, 512), BF16),
                vmem((2, LANES, 256), BF16),
                vmem((8, LANES), F32),
                vmem((CHUNKS, 8, 128), F32),
                vmem((2 * n_gy - 1, CHUNKS, 8, 128), F32),
                vmem((n_gx // 2 - 1, CHUNKS, 8, 128), F32),
                vmem((CHUNKS, 8, 128), F32),
                vmem((CHUNKS, 8, 128), F32),
                pltpu.SemaphoreType.DMA((11,)),
                pltpu.SemaphoreType.DMA((3,)),
                pltpu.SemaphoreType.DMA((4,)),
            ],
            compiler_params=pltpu.CompilerParams(
                collective_id=0, has_side_effects=True, vmem_limit_bytes=16 << 20
            ),
        )(*(pltpu.with_memory_space_constraint(array, pltpu.HBM) for array in arrays))

    placed = (
        P(None, "lev", "gy", "gx"),
        P(None, "lev"),
        P(None, "lev"),
        P("lev", None),
        P(("gx", "gy"), None, "lev", None),
    )
    return jax.shard_map(
        body, mesh=mesh, in_specs=placed, out_specs=P(None, "lev", "gy", "gx"), check_vma=False
    )
```

```python
import functools

import jax
import jax.numpy as jnp
import ml_dtypes
import numpy as np
from jax import lax
from jax.experimental import pallas as pl
from jax.experimental.pallas import tpu as pltpu
from jax.sharding import PartitionSpec as P

NX = 2048
NY = 2048
KC = 10
NK = 21
PAD = 24
WIDE = 32
FIELDS = 8
ROWS = NK * FIELDS
LANES = 512
CHUNKS = LANES // 128
ROOTS = (0, 8)
FAR = (12, 20)
MESH = pl.DeviceIdType.MESH
BF16 = jnp.bfloat16
F32 = jnp.float32


def split(table):
    high = table.astype(ml_dtypes.bfloat16)
    low = (table - high.astype(np.float64)).astype(ml_dtypes.bfloat16)
    return np.stack([high, low])


def wavenumbers():
    return np.concatenate([np.arange(KC + 1), np.arange(1, KC + 1)])


def basis(length):
    wave = wavenumbers()
    angle = 2.0 * np.pi * np.mod(wave[:, None] * np.arange(length)[None, :], length) / length
    is_cos = (np.arange(NK) <= KC)[:, None]
    return np.where(is_cos, np.cos(angle), np.sin(angle))


def along_y_tables(n_gy, fields):
    ny = NY // n_gy
    out = np.zeros((n_gy, PAD, fields * ny))
    out[:, :NK] = np.tile(basis(NY).reshape(NK, n_gy, ny).transpose(1, 0, 2), (1, 1, fields))
    high, low = split(out)
    return np.stack([high, low], axis=1)


def along_x_tables(n_gx):
    nx = NX // n_gx
    out = np.zeros((n_gx, WIDE, nx))
    out[:, :NK] = basis(NX).reshape(NK, n_gx, nx).transpose(1, 0, 2)
    high, low = split(out)
    return np.stack([high, low], axis=1)


def pick_table():
    out = np.zeros((WIDE, LANES))
    p = np.arange(NK * NK)
    out[p % NK, p] = 1.0
    return out.astype(ml_dtypes.bfloat16)


def fold_tables():
    wave = np.arange(NK) - KC
    number = wavenumbers()
    is_cos = np.arange(NK) <= KC
    hit = (number[:, None] == np.abs(wave)[None, :]).astype(np.float64)
    factor = np.where(is_cos[:, None], hit, hit * np.sign(wave)[None, :])
    table = np.zeros((NK * NK, LANES))
    table[:, : NK * NK] = np.einsum("ak,bj->kjab", factor, factor).reshape(NK * NK, NK * NK)
    both_cos = np.outer(is_cos, is_cos)
    both_sin = np.outer(~is_cos, ~is_cos)
    twice = np.where(number == 0, 1.0, 2.0)
    kinds = [
        np.outer(twice, twice) / (NX * NY),
        number[:, None] ** 2 + number[None, :] ** 2,
        both_cos.astype(np.float64) - both_sin.astype(np.float64),
        -(~(both_cos | both_sin)).astype(np.float64),
    ]
    rows = np.zeros((4, FIELDS, LANES), np.float32)
    for kind, value in enumerate(kinds):
        rows[kind, :, : NK * NK] = value.reshape(-1)
    return table.astype(ml_dtypes.bfloat16), rows.reshape(4 * FIELDS, LANES)


def halves(value):
    high = value.astype(BF16)
    low = (value - high.astype(F32)).astype(BF16)
    return high, low


def dot(left, right):
    return lax.dot_general(left, right, (((1,), (0,)), ((), ())), preferred_element_type=F32)


def dot_t(left, right):
    return lax.dot_general(left, right, (((1,), (1,)), ((), ())), preferred_element_type=F32)


def blocks(table):
    shape = (FIELDS, 2 * table.shape[2])
    field = lax.broadcasted_iota(jnp.int32, shape, 0)
    lane = lax.broadcasted_iota(jnp.int32, shape, 1)
    width = shape[1] // FIELDS
    keep = (lane >= field * width) & (lane < (field + 1) * width)
    out = []
    for part in range(2):
        half = table[part].astype(F32)
        whole = jnp.concatenate([half, half], axis=1)[:NK]
        out.append(jnp.where(keep[None], whole[:, None, :], 0.0).reshape(ROWS, shape[1]))
    return out


def dot_0(left, right):
    return lax.dot_general(left, right, (((0,), (0,)), ((), ())), preferred_element_type=F32)


def along_y(block, both_tables, high_table):
    high, low = halves(block)
    both = dot(both_tables, high)
    return both[:ROWS] + both[ROWS:] + dot(high_table, low)


def spans(a):
    return [
        (t, max(a * NK - 128 * t, 0), min((a + 1) * NK - 128 * t, 128))
        for t in range(a * NK // 128, (a * NK + NK - 1) // 128 + 1)
    ]


def along_x(value, table, pick):
    high, low = halves(value)
    narrow = dot_t(high, table[0]) + dot_t(high, table[1]) + dot_t(low, table[0])
    high, low = halves(narrow)
    wide = dot(high, pick) + dot(low, pick)
    lane = lax.broadcasted_iota(jnp.int32, (FIELDS, 128), 1)
    tiles = [None] * CHUNKS
    for a in range(NK):
        for t, start, _ in spans(a):
            here = wide[a * FIELDS : (a + 1) * FIELDS, t * 128 : (t + 1) * 128]
            tiles[t] = here if tiles[t] is None else jnp.where(lane >= start, here, tiles[t])
    return jnp.concatenate(tiles, axis=1)


def folded(era, table, sign_re, sign_im):
    parts = []
    for part in range(2):
        value = era[:, part * NK * NK : (part + 1) * NK * NK]
        first = value.astype(BF16).astype(F32)
        rest = value - first
        second = rest.astype(BF16).astype(F32)
        parts += [first, second, rest - second]
    out = dot(jnp.concatenate(parts, axis=0).astype(BF16), table)
    real = out[0:8] + out[8:16] + out[16:24]
    imag = out[24:32] + out[32:40] + out[40:48]
    return sign_re * real + sign_im * imag


def spread(coefs):
    lane = lax.broadcasted_iota(jnp.int32, (FIELDS, 128), 1)
    zero = jnp.zeros((FIELDS, 128), F32)
    rows = []
    for a in range(NK):
        tiles = [zero] * CHUNKS
        for t, start, stop in spans(a):
            tiles[t] = jnp.where((lane >= start) & (lane < stop), coefs[:, t * 128 : (t + 1) * 128], 0.0)
        rows.append(jnp.concatenate(tiles, axis=1))
    return jnp.concatenate(rows, axis=0)


def back_x(coefs, table):
    first = coefs.astype(BF16).astype(F32)
    high = spread(first)
    both = dot(jnp.concatenate([high, spread(coefs - first)], axis=0).astype(BF16), table[0])
    return both[:ROWS] + both[ROWS:] + dot(high.astype(BF16), table[1])


def back_y_tables(high, low):
    fill = jnp.zeros((512 - 3 * ROWS, high.shape[1]), F32)
    return jnp.concatenate([high, low, high, fill], axis=0).T.astype(BF16)


def back_y(value, table):
    high = value.astype(BF16).astype(F32)
    fill = jnp.zeros((512 - 3 * ROWS, value.shape[1]), F32)
    return dot(table, jnp.concatenate([high, high, value - high, fill], axis=0).astype(BF16))


def way_back():
    children = {
        (0, 0): [(0, 1), (1, 1), (4, 0), (1, 0), (3, 1), (2, 1), (3, 0), (2, 0)],
        (0, 1): [(31, 0)],
        (8, 0): [(8, 1), (5, 0), (5, 1), (6, 0), (6, 1), (7, 0), (12, 0), (9, 0), (10, 0), (11, 0)],
        (12, 0): [(12, 1), (13, 0), (14, 0), (15, 0)],
        (19, 0): [(19, 1), (16, 0), (17, 0), (18, 0)],
        (23, 0): [(23, 1), (20, 0), (21, 0), (22, 0)],
        (31, 0): [(31, 1), (19, 0), (23, 0)] + [(z, 0) for z in range(24, 31)],
    }
    parent = {child: node for node, nodes in children.items() for child in nodes}
    for z in range(1, 32):
        if (z, 1) not in parent:
            parent[z, 1] = (z, 0)
            children[z, 0] = [(z, 1)]
    return children, parent


def kernel(
    n_y, n_z,
    cutoff_in, relax_in, owner_in, state, era, tab_y, tab_x, tab_pick, tab_fold, tab_rows,
    out,
    cutoff, relax, owner, st, er, ty, tx, pick, fold, rows, by, tx_wide, scale, pay, got, got_y, mine_y, total,
    in_sem, send_sem, recv_sem,
):
    gx = lax.axis_index("gx")
    gz = lax.axis_index("gy")
    lev = lax.axis_index("lev")
    y = gx // 2
    children, parent = way_back()

    def swapped(y_pos):
        return jnp.where(jnp.logical_and(y_pos == 0, lev == 0), 1, 0)

    def at(y_pos, z_pos, slot):
        flip = swapped(y_pos)
        other = slot + flip - 2 * slot * flip
        return {"gx": y_pos * 2 + jnp.where(z_pos == 0, other, slot), "gy": z_pos}

    flip = swapped(y)
    core = gx % 2
    slot = jnp.where(gz == 0, core + flip - 2 * core * flip, core)
    index = 2 * gz + slot
    is_root = functools.reduce(jnp.logical_or, [index == 2 * r for r in ROOTS])

    def by_index(table, default):
        value = jnp.int32(default)
        for key, entry in table.items():
            if entry != default:
                value = jnp.where(index == 2 * key[0] + key[1], entry, value)
        return value

    copies = [
        pltpu.make_async_copy(tab_y.at[gz], ty, in_sem.at[0]),
        pltpu.make_async_copy(state.at[0], st.at[pl.ds(0, 4)], in_sem.at[1]),
        pltpu.make_async_copy(state.at[1], st.at[pl.ds(4, 4)], in_sem.at[2]),
        pltpu.make_async_copy(tab_x.at[gx], tx, in_sem.at[3]),
        pltpu.make_async_copy(tab_pick, pick, in_sem.at[4]),
        pltpu.make_async_copy(era.at[0], er, in_sem.at[5]),
        pltpu.make_async_copy(tab_fold, fold, in_sem.at[6]),
        pltpu.make_async_copy(tab_rows, rows, in_sem.at[7]),
        pltpu.make_async_copy(owner_in, owner, in_sem.at[8]),
        pltpu.make_async_copy(cutoff_in, cutoff, in_sem.at[9]),
        pltpu.make_async_copy(relax_in, relax, in_sem.at[10]),
    ]
    for copy in copies:
        copy.start()

    barrier = pltpu.get_barrier_semaphore()

    @pl.when(is_root)
    def _():
        def greet(i, carry):
            there = (gz + n_z // 4 + i // 2) % n_z

            @pl.when(2 * there + i % 2 != index)
            def _():
                pl.semaphore_signal(barrier, inc=1, device_id=at(y, there, i % 2), device_id_type=MESH)

            return carry

        lax.fori_loop(0, 2 * n_z, greet, 0)
        for step in range(1, n_y):
            pl.semaphore_signal(barrier, inc=1, device_id=at((y + step) % n_y, gz, 0), device_id_type=MESH)

    @pl.when(jnp.logical_not(is_root))
    def _():
        parent_z = by_index({key: node[0] for key, node in parent.items() if node[0] != key[0]}, -1)
        parent_z = jnp.where(parent_z < 0, gz, parent_z)
        parent_slot = by_index({key: node[1] for key, node in parent.items()}, 0)
        pl.semaphore_signal(barrier, inc=1, device_id=at(y, parent_z, parent_slot), device_id_type=MESH)

    copies[0].wait()
    y_high, y_low = blocks(ty[...])
    y_both = jnp.concatenate([y_high, y_low], axis=0).astype(BF16)
    copies[1].wait()
    copies[2].wait()
    along = along_y(st[...].reshape(512, 256), y_both, y_high.astype(BF16))
    copies[3].wait()
    copies[4].wait()
    partial = along_x(along, tx[...], pick[...])
    for copy in copies[5:]:
        copy.wait()
    held = folded(jnp.concatenate([er[0], er[1]], axis=0), fold[...], rows[16:24], rows[24:32])
    row = lax.broadcasted_iota(jnp.int32, (8, LANES), 0)
    me = gx * n_z + gz
    keeper = jnp.where(row < 4, owner[0, 0], owner[0, 1])
    share = jnp.where(keeper == me, held, 0.0) - rows[0:8] * partial
    for c in range(CHUNKS):
        pay[c] = share[:, c * 128 : (c + 1) * 128]

    def prepare():
        rate = jnp.zeros((8, LANES), F32)
        limit = jnp.zeros((8, LANES), jnp.int32)
        for f in range(8):
            rate = jnp.where(row == f, relax[f // 4, f % 4], rate)
            limit = jnp.where(row == f, cutoff[f // 4, f % 4], limit)
        scale[...] = jnp.where(rows[8:16] <= (limit * limit).astype(F32), rate, 0.0)
        for part in range(2):
            tx_wide[part] = dot_0(pick[...], tx[part]).astype(BF16)
        by[...] = back_y_tables(y_high, y_low)

    n_far = 2 * (FAR[1] - FAR[0])
    n_near = 2 * n_z - 1 - n_far

    def remote(src, dst, which, target):
        return pltpu.make_async_remote_copy(
            src, dst, send_sem.at[which % 3], recv_sem.at[which], device_id=target, device_id_type=MESH
        )

    root = at(y, 16, 0)
    n_children = by_index({key: len(nodes) for key, nodes in children.items()}, 0)
    busy = [key for key, nodes in children.items() if key == (0, 1) or len(nodes) > 1]
    top = [(r, 0) for r in ROOTS]
    is_relay = jnp.logical_and(slot == 0, n_children == 1)

    def pass_on(key):
        for z, child_slot in children[key]:
            remote(total, total, 2, at(y, z, child_slot)).start()

    pl.semaphore_wait(barrier, n_children + jnp.where(is_root, len(ROOTS) + n_y - 2, len(ROOTS)))
    for r in ROOTS:
        from_root = (index + 2 * n_z - 2 * r) % (2 * n_z)
        far = jnp.logical_and(from_root >= 2 * FAR[0], from_root < 2 * FAR[1])
        after = jnp.where(from_root >= 2 * FAR[1], from_root - n_far, from_root) - 1
        place = jnp.where(far, n_near + from_root - 2 * FAR[0], after)

        @pl.when(index != 2 * r)
        def _():
            pltpu.make_async_remote_copy(
                pay, got.at[place], send_sem.at[0], recv_sem.at[jnp.where(far, 3, 0)],
                device_id=at(y, r, 0), device_id_type=MESH,
            ).start()

    prepare()

    @pl.when(jnp.logical_not(is_root))
    def _():
        remote(total, total, 2, root).wait_recv()

    @pl.when(is_root)
    def _():
        near, far = got.at[pl.ds(0, n_near)], got.at[pl.ds(n_near, n_far)]
        remote(near, near, 0, root).wait_recv()
        first = pay[...] + jnp.sum(near[...], axis=0)
        remote(far, far, 3, root).wait_recv()
        mine_y[...] = first + jnp.sum(far[...], axis=0)
        for step in range(1, n_y):
            remote(mine_y, got_y.at[step - 1], 1, at((y + step) % n_y, gz, 0)).start()
        remote(got_y, got_y, 1, root).wait_recv()
        total[...] = mine_y[...] + jnp.sum(got_y[...], axis=0)

    for key in top + [key for key in busy if key not in top]:
        pl.when(index == 2 * key[0] + key[1])(functools.partial(pass_on, key))

    @pl.when(is_relay)
    def _():
        remote(total, total, 2, at(y, gz, 1)).start()

    summed = jnp.concatenate([total[c] for c in range(CHUNKS)], axis=1)
    added = back_y(back_x(summed * scale[...], tx_wide[...]), by[...])
    for h in range(2):
        block = added[256 * h : 256 * (h + 1)].reshape(4, 64, 256)
        out[h] = st[4 * h : 4 * h + 4] + block

    def pass_on_sent(count):
        sent = got.at[pl.ds(0, count)]
        remote(sent, sent, 2, root).wait_send()

    def shares_sent(count):
        sent = got.at[pl.ds(0, count)]
        remote(sent, sent, 0, root).wait_send()

    @pl.when(is_root)
    def _():
        remote(got_y, got_y, 1, root).wait_send()
        shares_sent(len(ROOTS) - 1)

    @pl.when(jnp.logical_not(is_root))
    def _():
        shares_sent(len(ROOTS))

    for key in busy:
        pl.when(index == 2 * key[0] + key[1])(functools.partial(pass_on_sent, len(children[key])))

    @pl.when(is_relay)
    def _():
        pass_on_sent(1)


def solution(mesh):
    n_gx, n_gy = mesh.shape["gx"], mesh.shape["gy"]
    tables = (along_y_tables(n_gy, FIELDS // 2), along_x_tables(n_gx), pick_table(), *fold_tables())

    def body(model_state, cutoff, relax_rate, owner_map, era_store):
        arrays = (cutoff, relax_rate, owner_map, model_state, era_store, *(jnp.asarray(t) for t in tables))
        vmem = pltpu.VMEM
        return pl.pallas_call(
            functools.partial(kernel, n_gx // 2, n_gy),
            out_shape=jax.ShapeDtypeStruct(model_state.shape, F32),
            in_specs=[pl.BlockSpec(memory_space=pltpu.HBM)] * 10,
            out_specs=pl.BlockSpec(memory_space=vmem),
            scratch_shapes=[
                pltpu.SMEM((2, 4), jnp.int32),
                pltpu.SMEM((2, 4), F32),
                pltpu.SMEM((1, 2), jnp.int32),
                vmem((8, 64, 256), F32),
                vmem((2, 4, 2 * NK * NK), F32),
                vmem((2, PAD, 256), BF16),
                vmem((2, WIDE, 256), BF16),
                vmem((WIDE, LANES), BF16),
                vmem((NK * NK, LANES), BF16),
                vmem((4 * FIELDS, LANES), F32),
                vmem((512, 512), BF16),
                vmem((2, LANES, 256), BF16),
                vmem((8, LANES), F32),
                vmem((CHUNKS, 8, 128), F32),
                vmem((2 * n_gy - 1, CHUNKS, 8, 128), F32),
                vmem((n_gx // 2 - 1, CHUNKS, 8, 128), F32),
                vmem((CHUNKS, 8, 128), F32),
                vmem((CHUNKS, 8, 128), F32),
                pltpu.SemaphoreType.DMA((11,)),
                pltpu.SemaphoreType.DMA((3,)),
                pltpu.SemaphoreType.DMA((4,)),
            ],
            compiler_params=pltpu.CompilerParams(
                collective_id=0, has_side_effects=True, vmem_limit_bytes=16 << 20
            ),
        )(*(pltpu.with_memory_space_constraint(array, pltpu.HBM) for array in arrays))

    placed = (
        P(None, "lev", "gy", "gx"),
        P(None, "lev"),
        P(None, "lev"),
        P("lev", None),
        P(("gx", "gy"), None, "lev", None),
    )
    return jax.shard_map(
        body, mesh=mesh, in_specs=placed, out_specs=P(None, "lev", "gy", "gx"), check_vma=False
    )
```

```python
import functools

import jax
import jax.numpy as jnp
import ml_dtypes
import numpy as np
from jax import lax
from jax.experimental import pallas as pl
from jax.experimental.pallas import tpu as pltpu
from jax.sharding import PartitionSpec as P

NX = 2048
NY = 2048
KC = 10
NK = 21
PAD = 24
WIDE = 32
FIELDS = 8
ROWS = NK * FIELDS
LANES = 512
CHUNKS = LANES // 128
ROOTS = (0, 8)
FAR = (12, 20)
MESH = pl.DeviceIdType.MESH
BF16 = jnp.bfloat16
F32 = jnp.float32


def split(table):
    high = table.astype(ml_dtypes.bfloat16)
    low = (table - high.astype(np.float64)).astype(ml_dtypes.bfloat16)
    return np.stack([high, low])


def wavenumbers():
    return np.concatenate([np.arange(KC + 1), np.arange(1, KC + 1)])


def basis(length):
    wave = wavenumbers()
    angle = 2.0 * np.pi * np.mod(wave[:, None] * np.arange(length)[None, :], length) / length
    is_cos = (np.arange(NK) <= KC)[:, None]
    return np.where(is_cos, np.cos(angle), np.sin(angle))


def along_y_tables(n_gy, fields):
    ny = NY // n_gy
    out = np.zeros((n_gy, PAD, fields * ny))
    out[:, :NK] = np.tile(basis(NY).reshape(NK, n_gy, ny).transpose(1, 0, 2), (1, 1, fields))
    high, low = split(out)
    return np.stack([high, low], axis=1)


def along_x_tables(n_gx):
    nx = NX // n_gx
    out = np.zeros((n_gx, WIDE, nx))
    out[:, :NK] = basis(NX).reshape(NK, n_gx, nx).transpose(1, 0, 2)
    high, low = split(out)
    return np.stack([high, low], axis=1)


def pick_table():
    out = np.zeros((WIDE, LANES))
    p = np.arange(NK * NK)
    out[p % NK, p] = 1.0
    return out.astype(ml_dtypes.bfloat16)


def fold_tables():
    wave = np.arange(NK) - KC
    number = wavenumbers()
    is_cos = np.arange(NK) <= KC
    hit = (number[:, None] == np.abs(wave)[None, :]).astype(np.float64)
    factor = np.where(is_cos[:, None], hit, hit * np.sign(wave)[None, :])
    table = np.zeros((NK * NK, LANES))
    table[:, : NK * NK] = np.einsum("ak,bj->kjab", factor, factor).reshape(NK * NK, NK * NK)
    both_cos = np.outer(is_cos, is_cos)
    both_sin = np.outer(~is_cos, ~is_cos)
    twice = np.where(number == 0, 1.0, 2.0)
    kinds = [
        np.outer(twice, twice) / (NX * NY),
        number[:, None] ** 2 + number[None, :] ** 2,
        both_cos.astype(np.float64) - both_sin.astype(np.float64),
        -(~(both_cos | both_sin)).astype(np.float64),
    ]
    rows = np.zeros((4, FIELDS, LANES), np.float32)
    for kind, value in enumerate(kinds):
        rows[kind, :, : NK * NK] = value.reshape(-1)
    return table.astype(ml_dtypes.bfloat16), rows.reshape(4 * FIELDS, LANES)


def halves(value):
    high = value.astype(BF16)
    low = (value - high.astype(F32)).astype(BF16)
    return high, low


def dot(left, right):
    return lax.dot_general(left, right, (((1,), (0,)), ((), ())), preferred_element_type=F32)


def dot_t(left, right):
    return lax.dot_general(left, right, (((1,), (1,)), ((), ())), preferred_element_type=F32)


def blocks(table):
    shape = (FIELDS, 2 * table.shape[2])
    field = lax.broadcasted_iota(jnp.int32, shape, 0)
    lane = lax.broadcasted_iota(jnp.int32, shape, 1)
    width = shape[1] // FIELDS
    keep = (lane >= field * width) & (lane < (field + 1) * width)
    out = []
    for part in range(2):
        half = table[part].astype(F32)
        whole = jnp.concatenate([half, half], axis=1)[:NK]
        out.append(jnp.where(keep[None], whole[:, None, :], 0.0).reshape(ROWS, shape[1]))
    return out


def dot_0(left, right):
    return lax.dot_general(left, right, (((0,), (0,)), ((), ())), preferred_element_type=F32)


def along_y(block, both_tables, high_table):
    high, low = halves(block)
    both = dot(both_tables, high)
    return both[:ROWS] + both[ROWS:] + dot(high_table, low)


def spans(a):
    return [
        (t, max(a * NK - 128 * t, 0), min((a + 1) * NK - 128 * t, 128))
        for t in range(a * NK // 128, (a * NK + NK - 1) // 128 + 1)
    ]


def along_x(value, table, pick):
    high, low = halves(value)
    narrow = dot_t(high, table[0]) + dot_t(high, table[1]) + dot_t(low, table[0])
    high, low = halves(narrow)
    wide = dot(high, pick) + dot(low, pick)
    lane = lax.broadcasted_iota(jnp.int32, (FIELDS, 128), 1)
    tiles = [None] * CHUNKS
    for a in range(NK):
        for t, start, _ in spans(a):
            here = wide[a * FIELDS : (a + 1) * FIELDS, t * 128 : (t + 1) * 128]
            tiles[t] = here if tiles[t] is None else jnp.where(lane >= start, here, tiles[t])
    return jnp.concatenate(tiles, axis=1)


def folded(era, table, sign_re, sign_im):
    parts = []
    for part in range(2):
        value = era[:, part * NK * NK : (part + 1) * NK * NK]
        first = value.astype(BF16).astype(F32)
        rest = value - first
        second = rest.astype(BF16).astype(F32)
        parts += [first, second, rest - second]
    out = dot(jnp.concatenate(parts, axis=0).astype(BF16), table)
    real = out[0:8] + out[8:16] + out[16:24]
    imag = out[24:32] + out[32:40] + out[40:48]
    return sign_re * real + sign_im * imag


def spread(coefs):
    lane = lax.broadcasted_iota(jnp.int32, (FIELDS, 128), 1)
    zero = jnp.zeros((FIELDS, 128), F32)
    rows = []
    for a in range(NK):
        tiles = [zero] * CHUNKS
        for t, start, stop in spans(a):
            tiles[t] = jnp.where((lane >= start) & (lane < stop), coefs[:, t * 128 : (t + 1) * 128], 0.0)
        rows.append(jnp.concatenate(tiles, axis=1))
    return jnp.concatenate(rows, axis=0)


def back_x(coefs, table):
    first = coefs.astype(BF16).astype(F32)
    high = spread(first)
    both = dot(jnp.concatenate([high, spread(coefs - first)], axis=0).astype(BF16), table[0])
    return both[:ROWS] + both[ROWS:] + dot(high.astype(BF16), table[1])


def back_y_tables(high, low):
    fill = jnp.zeros((512 - 3 * ROWS, high.shape[1]), F32)
    return jnp.concatenate([high, low, high, fill], axis=0).T.astype(BF16)


def back_y(value, table):
    high = value.astype(BF16).astype(F32)
    fill = jnp.zeros((512 - 3 * ROWS, value.shape[1]), F32)
    return dot(table, jnp.concatenate([high, high, value - high, fill], axis=0).astype(BF16))


def way_back():
    children = {
        (0, 0): [(1, 1), (1, 0), (4, 0), (2, 1), (2, 0), (0, 1), (3, 1), (3, 0)],
        (0, 1): [(31, 0)],
        (8, 0): [(8, 1), (5, 0), (5, 1), (6, 0), (6, 1), (7, 0), (12, 0), (9, 0), (10, 0), (11, 0)],
        (12, 0): [(12, 1), (13, 0), (14, 0), (15, 0)],
        (19, 0): [(19, 1), (16, 0), (17, 0), (18, 0)],
        (23, 0): [(23, 1), (20, 0), (21, 0), (22, 0)],
        (31, 0): [(31, 1), (19, 0), (23, 0)] + [(z, 0) for z in range(24, 31)],
    }
    parent = {child: node for node, nodes in children.items() for child in nodes}
    for z in range(1, 32):
        if (z, 1) not in parent:
            parent[z, 1] = (z, 0)
            children[z, 0] = [(z, 1)]
    return children, parent


def kernel(
    n_y, n_z,
    cutoff_in, relax_in, owner_in, state, era, tab_y, tab_x, tab_pick, tab_fold, tab_rows,
    out,
    cutoff, relax, owner, st, er, ty, tx, pick, fold, rows, by, tx_wide, scale, pay, got, got_y, mine_y, total,
    in_sem, send_sem, recv_sem,
):
    gx = lax.axis_index("gx")
    gz = lax.axis_index("gy")
    lev = lax.axis_index("lev")
    y = gx // 2
    children, parent = way_back()

    def swapped(y_pos):
        return jnp.where(jnp.logical_and(y_pos == 0, lev == 0), 1, 0)

    def at(y_pos, z_pos, slot):
        flip = swapped(y_pos)
        other = slot + flip - 2 * slot * flip
        return {"gx": y_pos * 2 + jnp.where(z_pos == 0, other, slot), "gy": z_pos}

    flip = swapped(y)
    core = gx % 2
    slot = jnp.where(gz == 0, core + flip - 2 * core * flip, core)
    index = 2 * gz + slot
    is_root = functools.reduce(jnp.logical_or, [index == 2 * r for r in ROOTS])

    def by_index(table, default):
        value = jnp.int32(default)
        for key, entry in table.items():
            if entry != default:
                value = jnp.where(index == 2 * key[0] + key[1], entry, value)
        return value

    copies = [
        pltpu.make_async_copy(tab_y.at[gz], ty, in_sem.at[0]),
        pltpu.make_async_copy(state.at[0], st.at[pl.ds(0, 4)], in_sem.at[1]),
        pltpu.make_async_copy(state.at[1], st.at[pl.ds(4, 4)], in_sem.at[2]),
        pltpu.make_async_copy(tab_x.at[gx], tx, in_sem.at[3]),
        pltpu.make_async_copy(tab_pick, pick, in_sem.at[4]),
        pltpu.make_async_copy(era.at[0], er, in_sem.at[5]),
        pltpu.make_async_copy(tab_fold, fold, in_sem.at[6]),
        pltpu.make_async_copy(tab_rows, rows, in_sem.at[7]),
        pltpu.make_async_copy(owner_in, owner, in_sem.at[8]),
        pltpu.make_async_copy(cutoff_in, cutoff, in_sem.at[9]),
        pltpu.make_async_copy(relax_in, relax, in_sem.at[10]),
    ]
    for copy in copies:
        copy.start()

    barrier = pltpu.get_barrier_semaphore()

    @pl.when(is_root)
    def _():
        def greet(i, carry):
            there = (gz + n_z // 4 + i // 2) % n_z

            @pl.when(2 * there + i % 2 != index)
            def _():
                pl.semaphore_signal(barrier, inc=1, device_id=at(y, there, i % 2), device_id_type=MESH)

            return carry

        lax.fori_loop(0, 2 * n_z, greet, 0)
        for step in range(1, n_y):
            pl.semaphore_signal(barrier, inc=1, device_id=at((y + step) % n_y, gz, 0), device_id_type=MESH)

    @pl.when(jnp.logical_not(is_root))
    def _():
        parent_z = by_index({key: node[0] for key, node in parent.items() if node[0] != key[0]}, -1)
        parent_z = jnp.where(parent_z < 0, gz, parent_z)
        parent_slot = by_index({key: node[1] for key, node in parent.items()}, 0)
        pl.semaphore_signal(barrier, inc=1, device_id=at(y, parent_z, parent_slot), device_id_type=MESH)

    copies[0].wait()
    y_high, y_low = blocks(ty[...])
    y_both = jnp.concatenate([y_high, y_low], axis=0).astype(BF16)
    copies[1].wait()
    copies[2].wait()
    along = along_y(st[...].reshape(512, 256), y_both, y_high.astype(BF16))
    for copy in copies[3:]:
        copy.wait()
    partial = along_x(along, tx[...], pick[...])
    held = folded(jnp.concatenate([er[0], er[1]], axis=0), fold[...], rows[16:24], rows[24:32])
    row = lax.broadcasted_iota(jnp.int32, (8, LANES), 0)
    me = gx * n_z + gz
    keeper = jnp.where(row < 4, owner[0, 0], owner[0, 1])
    share = jnp.where(keeper == me, held, 0.0) - rows[0:8] * partial
    for c in range(CHUNKS):
        pay[c] = share[:, c * 128 : (c + 1) * 128]

    def prepare():
        rate = jnp.zeros((8, LANES), F32)
        limit = jnp.zeros((8, LANES), jnp.int32)
        for f in range(8):
            rate = jnp.where(row == f, relax[f // 4, f % 4], rate)
            limit = jnp.where(row == f, cutoff[f // 4, f % 4], limit)
        scale[...] = jnp.where(rows[8:16] <= (limit * limit).astype(F32), rate, 0.0)
        for part in range(2):
            tx_wide[part] = dot_0(pick[...], tx[part]).astype(BF16)
        by[...] = back_y_tables(y_high, y_low)

    n_far = 2 * (FAR[1] - FAR[0])
    n_near = 2 * n_z - 1 - n_far

    def remote(src, dst, which, target):
        return pltpu.make_async_remote_copy(
            src, dst, send_sem.at[which % 3], recv_sem.at[which], device_id=target, device_id_type=MESH
        )

    root = at(y, 16, 0)
    n_children = by_index({key: len(nodes) for key, nodes in children.items()}, 0)
    busy = [key for key, nodes in children.items() if key == (0, 1) or len(nodes) > 1]
    top = [(r, 0) for r in ROOTS]
    is_relay = jnp.logical_and(slot == 0, n_children == 1)

    def pass_on(key):
        for z, child_slot in children[key]:
            remote(total, total, 2, at(y, z, child_slot)).start()

    pl.semaphore_wait(barrier, n_children + jnp.where(is_root, len(ROOTS) + n_y - 2, len(ROOTS)))
    for r in ROOTS:
        from_root = (index + 2 * n_z - 2 * r) % (2 * n_z)
        far = jnp.logical_and(from_root >= 2 * FAR[0], from_root < 2 * FAR[1])
        after = jnp.where(from_root >= 2 * FAR[1], from_root - n_far, from_root) - 1
        place = jnp.where(far, n_near + from_root - 2 * FAR[0], after)

        @pl.when(index != 2 * r)
        def _():
            pltpu.make_async_remote_copy(
                pay, got.at[place], send_sem.at[0], recv_sem.at[jnp.where(far, 3, 0)],
                device_id=at(y, r, 0), device_id_type=MESH,
            ).start()

    prepare()

    @pl.when(jnp.logical_not(is_root))
    def _():
        remote(total, total, 2, root).wait_recv()

    @pl.when(is_root)
    def _():
        near, far = got.at[pl.ds(0, n_near)], got.at[pl.ds(n_near, n_far)]
        remote(near, near, 0, root).wait_recv()
        first = pay[...] + jnp.sum(near[...], axis=0)
        remote(far, far, 3, root).wait_recv()
        mine_y[...] = first + jnp.sum(far[...], axis=0)
        for step in sorted(range(1, n_y), key=lambda step: -min(step, n_y - step)):
            remote(mine_y, got_y.at[step - 1], 1, at((y + step) % n_y, gz, 0)).start()
        remote(got_y, got_y, 1, root).wait_recv()
        total[...] = mine_y[...] + jnp.sum(got_y[...], axis=0)

    for key in top + [key for key in busy if key not in top]:
        pl.when(index == 2 * key[0] + key[1])(functools.partial(pass_on, key))

    @pl.when(is_relay)
    def _():
        remote(total, total, 2, at(y, gz, 1)).start()

    summed = jnp.concatenate([total[c] for c in range(CHUNKS)], axis=1)
    added = back_y(back_x(summed * scale[...], tx_wide[...]), by[...])
    for h in range(2):
        block = added[256 * h : 256 * (h + 1)].reshape(4, 64, 256)
        out[h] = st[4 * h : 4 * h + 4] + block

    def pass_on_sent(count):
        sent = got.at[pl.ds(0, count)]
        remote(sent, sent, 2, root).wait_send()

    def shares_sent(count):
        sent = got.at[pl.ds(0, count)]
        remote(sent, sent, 0, root).wait_send()

    @pl.when(is_root)
    def _():
        remote(got_y, got_y, 1, root).wait_send()
        shares_sent(len(ROOTS) - 1)

    @pl.when(jnp.logical_not(is_root))
    def _():
        shares_sent(len(ROOTS))

    for key in busy:
        pl.when(index == 2 * key[0] + key[1])(functools.partial(pass_on_sent, len(children[key])))

    @pl.when(is_relay)
    def _():
        pass_on_sent(1)


def solution(mesh):
    n_gx, n_gy = mesh.shape["gx"], mesh.shape["gy"]
    tables = (along_y_tables(n_gy, FIELDS // 2), along_x_tables(n_gx), pick_table(), *fold_tables())

    def body(model_state, cutoff, relax_rate, owner_map, era_store):
        arrays = (cutoff, relax_rate, owner_map, model_state, era_store, *(jnp.asarray(t) for t in tables))
        vmem = pltpu.VMEM
        return pl.pallas_call(
            functools.partial(kernel, n_gx // 2, n_gy),
            out_shape=jax.ShapeDtypeStruct(model_state.shape, F32),
            in_specs=[pl.BlockSpec(memory_space=pltpu.HBM)] * 10,
            out_specs=pl.BlockSpec(memory_space=vmem),
            scratch_shapes=[
                pltpu.SMEM((2, 4), jnp.int32),
                pltpu.SMEM((2, 4), F32),
                pltpu.SMEM((1, 2), jnp.int32),
                vmem((8, 64, 256), F32),
                vmem((2, 4, 2 * NK * NK), F32),
                vmem((2, PAD, 256), BF16),
                vmem((2, WIDE, 256), BF16),
                vmem((WIDE, LANES), BF16),
                vmem((NK * NK, LANES), BF16),
                vmem((4 * FIELDS, LANES), F32),
                vmem((512, 512), BF16),
                vmem((2, LANES, 256), BF16),
                vmem((8, LANES), F32),
                vmem((CHUNKS, 8, 128), F32),
                vmem((2 * n_gy - 1, CHUNKS, 8, 128), F32),
                vmem((n_gx // 2 - 1, CHUNKS, 8, 128), F32),
                vmem((CHUNKS, 8, 128), F32),
                vmem((CHUNKS, 8, 128), F32),
                pltpu.SemaphoreType.DMA((11,)),
                pltpu.SemaphoreType.DMA((3,)),
                pltpu.SemaphoreType.DMA((4,)),
            ],
            compiler_params=pltpu.CompilerParams(
                collective_id=0, has_side_effects=True, vmem_limit_bytes=16 << 20
            ),
        )(*(pltpu.with_memory_space_constraint(array, pltpu.HBM) for array in arrays))

    placed = (
        P(None, "lev", "gy", "gx"),
        P(None, "lev"),
        P(None, "lev"),
        P("lev", None),
        P(("gx", "gy"), None, "lev", None),
    )
    return jax.shard_map(
        body, mesh=mesh, in_specs=placed, out_specs=P(None, "lev", "gy", "gx"), check_vma=False
    )
```

```python
import functools

import jax
import jax.numpy as jnp
import ml_dtypes
import numpy as np
from jax import lax
from jax.experimental import pallas as pl
from jax.experimental.pallas import tpu as pltpu
from jax.sharding import PartitionSpec as P

NX = 2048
NY = 2048
KC = 10
NK = 21
PAD = 24
WIDE = 32
FIELDS = 8
ROWS = NK * FIELDS
LANES = 512
CHUNKS = LANES // 128
ROOTS = (0, 8)
FAR = (12, 20)
MESH = pl.DeviceIdType.MESH
BF16 = jnp.bfloat16
F32 = jnp.float32


def split(table):
    high = table.astype(ml_dtypes.bfloat16)
    low = (table - high.astype(np.float64)).astype(ml_dtypes.bfloat16)
    return np.stack([high, low])


def wavenumbers():
    return np.concatenate([np.arange(KC + 1), np.arange(1, KC + 1)])


def basis(length):
    wave = wavenumbers()
    angle = 2.0 * np.pi * np.mod(wave[:, None] * np.arange(length)[None, :], length) / length
    is_cos = (np.arange(NK) <= KC)[:, None]
    return np.where(is_cos, np.cos(angle), np.sin(angle))


def along_y_tables(n_gy, fields):
    ny = NY // n_gy
    out = np.zeros((n_gy, PAD, fields * ny))
    out[:, :NK] = np.tile(basis(NY).reshape(NK, n_gy, ny).transpose(1, 0, 2), (1, 1, fields))
    high, low = split(out)
    return np.stack([high, low], axis=1)


def along_x_tables(n_gx):
    nx = NX // n_gx
    out = np.zeros((n_gx, WIDE, nx))
    out[:, :NK] = basis(NX).reshape(NK, n_gx, nx).transpose(1, 0, 2)
    high, low = split(out)
    return np.stack([high, low], axis=1)


def pick_table():
    out = np.zeros((WIDE, LANES))
    p = np.arange(NK * NK)
    out[p % NK, p] = 1.0
    return out.astype(ml_dtypes.bfloat16)


def fold_tables():
    wave = np.arange(NK) - KC
    number = wavenumbers()
    is_cos = np.arange(NK) <= KC
    hit = (number[:, None] == np.abs(wave)[None, :]).astype(np.float64)
    factor = np.where(is_cos[:, None], hit, hit * np.sign(wave)[None, :])
    table = np.zeros((NK * NK, LANES))
    table[:, : NK * NK] = np.einsum("ak,bj->kjab", factor, factor).reshape(NK * NK, NK * NK)
    both_cos = np.outer(is_cos, is_cos)
    both_sin = np.outer(~is_cos, ~is_cos)
    twice = np.where(number == 0, 1.0, 2.0)
    kinds = [
        np.outer(twice, twice) / (NX * NY),
        number[:, None] ** 2 + number[None, :] ** 2,
        both_cos.astype(np.float64) - both_sin.astype(np.float64),
        -(~(both_cos | both_sin)).astype(np.float64),
    ]
    rows = np.zeros((4, FIELDS, LANES), np.float32)
    for kind, value in enumerate(kinds):
        rows[kind, :, : NK * NK] = value.reshape(-1)
    return table.astype(ml_dtypes.bfloat16), rows.reshape(4 * FIELDS, LANES)


def halves(value):
    high = value.astype(BF16)
    low = (value - high.astype(F32)).astype(BF16)
    return high, low


def dot(left, right):
    return lax.dot_general(left, right, (((1,), (0,)), ((), ())), preferred_element_type=F32)


def dot_t(left, right):
    return lax.dot_general(left, right, (((1,), (1,)), ((), ())), preferred_element_type=F32)


def blocks(table):
    shape = (FIELDS, 2 * table.shape[2])
    field = lax.broadcasted_iota(jnp.int32, shape, 0)
    lane = lax.broadcasted_iota(jnp.int32, shape, 1)
    width = shape[1] // FIELDS
    keep = (lane >= field * width) & (lane < (field + 1) * width)
    out = []
    for part in range(2):
        half = table[part].astype(F32)
        whole = jnp.concatenate([half, half], axis=1)[:NK]
        out.append(jnp.where(keep[None], whole[:, None, :], 0.0).reshape(ROWS, shape[1]))
    return out


def dot_0(left, right):
    return lax.dot_general(left, right, (((0,), (0,)), ((), ())), preferred_element_type=F32)


def along_y(block, both_tables, high_table):
    high, low = halves(block)
    both = dot(both_tables, high)
    return both[:ROWS] + both[ROWS:] + dot(high_table, low)


def spans(a):
    return [
        (t, max(a * NK - 128 * t, 0), min((a + 1) * NK - 128 * t, 128))
        for t in range(a * NK // 128, (a * NK + NK - 1) // 128 + 1)
    ]


def along_x(value, high_table, low_table):
    high, low = halves(value)
    wide = dot(high, high_table) + dot(high, low_table) + dot(low, high_table)
    lane = lax.broadcasted_iota(jnp.int32, (FIELDS, 128), 1)
    tiles = [None] * CHUNKS
    for a in range(NK):
        for t, start, _ in spans(a):
            here = wide[a * FIELDS : (a + 1) * FIELDS, t * 128 : (t + 1) * 128]
            tiles[t] = here if tiles[t] is None else jnp.where(lane >= start, here, tiles[t])
    return jnp.concatenate(tiles, axis=1)


def folded(era, table, sign_re, sign_im):
    parts = []
    for part in range(2):
        value = era[:, part * NK * NK : (part + 1) * NK * NK]
        first = value.astype(BF16).astype(F32)
        rest = value - first
        second = rest.astype(BF16).astype(F32)
        parts += [first, second, rest - second]
    out = dot(jnp.concatenate(parts, axis=0).astype(BF16), table)
    real = out[0:8] + out[8:16] + out[16:24]
    imag = out[24:32] + out[32:40] + out[40:48]
    return sign_re * real + sign_im * imag


def spread(coefs):
    lane = lax.broadcasted_iota(jnp.int32, (FIELDS, 128), 1)
    zero = jnp.zeros((FIELDS, 128), F32)
    rows = []
    for a in range(NK):
        tiles = [zero] * CHUNKS
        for t, start, stop in spans(a):
            tiles[t] = jnp.where((lane >= start) & (lane < stop), coefs[:, t * 128 : (t + 1) * 128], 0.0)
        rows.append(jnp.concatenate(tiles, axis=1))
    return jnp.concatenate(rows, axis=0)


def back_x(coefs, table):
    first = coefs.astype(BF16).astype(F32)
    high = spread(first)
    both = dot(jnp.concatenate([high, spread(coefs - first)], axis=0).astype(BF16), table[0])
    return both[:ROWS] + both[ROWS:] + dot(high.astype(BF16), table[1])


def back_y_tables(high, low):
    fill = jnp.zeros((512 - 3 * ROWS, high.shape[1]), F32)
    return jnp.concatenate([high, low, high, fill], axis=0).T.astype(BF16)


def back_y(value, table):
    high = value.astype(BF16).astype(F32)
    fill = jnp.zeros((512 - 3 * ROWS, value.shape[1]), F32)
    return dot(table, jnp.concatenate([high, high, value - high, fill], axis=0).astype(BF16))


def way_back():
    children = {
        (0, 0): [(1, 1), (1, 0), (4, 0), (2, 1), (2, 0), (0, 1), (3, 1), (3, 0)],
        (0, 1): [(31, 0)],
        (8, 0): [(8, 1), (5, 0), (5, 1), (6, 0), (6, 1), (7, 0), (12, 0), (9, 0), (10, 0), (11, 0)],
        (12, 0): [(12, 1), (13, 0), (14, 0), (15, 0)],
        (19, 0): [(19, 1), (16, 0), (17, 0), (18, 0)],
        (23, 0): [(23, 1), (20, 0), (21, 0), (22, 0)],
        (31, 0): [(31, 1), (19, 0), (23, 0)] + [(z, 0) for z in range(24, 31)],
    }
    parent = {child: node for node, nodes in children.items() for child in nodes}
    for z in range(1, 32):
        if (z, 1) not in parent:
            parent[z, 1] = (z, 0)
            children[z, 0] = [(z, 1)]
    return children, parent


def kernel(
    n_y, n_z,
    cutoff_in, relax_in, owner_in, state, era, tab_y, tab_x, tab_pick, tab_fold, tab_rows,
    out,
    cutoff, relax, owner, st, er, ty, tx, pick, fold, rows, by, tx_wide, scale, pay, got, got_y, mine_y, total,
    in_sem, send_sem, recv_sem,
):
    gx = lax.axis_index("gx")
    gz = lax.axis_index("gy")
    lev = lax.axis_index("lev")
    y = gx // 2
    children, parent = way_back()

    def swapped(y_pos):
        return jnp.where(jnp.logical_and(y_pos == 0, lev == 0), 1, 0)

    def at(y_pos, z_pos, slot):
        flip = swapped(y_pos)
        other = slot + flip - 2 * slot * flip
        return {"gx": y_pos * 2 + jnp.where(z_pos == 0, other, slot), "gy": z_pos}

    flip = swapped(y)
    core = gx % 2
    slot = jnp.where(gz == 0, core + flip - 2 * core * flip, core)
    index = 2 * gz + slot
    is_root = functools.reduce(jnp.logical_or, [index == 2 * r for r in ROOTS])

    def by_index(table, default):
        value = jnp.int32(default)
        for key, entry in table.items():
            if entry != default:
                value = jnp.where(index == 2 * key[0] + key[1], entry, value)
        return value

    copies = [
        pltpu.make_async_copy(tab_y.at[gz], ty, in_sem.at[0]),
        pltpu.make_async_copy(state.at[0], st.at[pl.ds(0, 4)], in_sem.at[1]),
        pltpu.make_async_copy(state.at[1], st.at[pl.ds(4, 4)], in_sem.at[2]),
        pltpu.make_async_copy(tab_x.at[gx], tx, in_sem.at[3]),
        pltpu.make_async_copy(tab_pick, pick, in_sem.at[4]),
        pltpu.make_async_copy(era.at[0], er, in_sem.at[5]),
        pltpu.make_async_copy(tab_fold, fold, in_sem.at[6]),
        pltpu.make_async_copy(tab_rows, rows, in_sem.at[7]),
        pltpu.make_async_copy(owner_in, owner, in_sem.at[8]),
        pltpu.make_async_copy(cutoff_in, cutoff, in_sem.at[9]),
        pltpu.make_async_copy(relax_in, relax, in_sem.at[10]),
    ]
    for copy in [copies[i] for i in (0, 3, 4, 1, 2, 5, 6, 7, 8, 9, 10)]:
        copy.start()

    barrier = pltpu.get_barrier_semaphore()

    @pl.when(is_root)
    def _():
        def greet(i, carry):
            there = (gz + n_z // 4 + i // 2) % n_z

            @pl.when(2 * there + i % 2 != index)
            def _():
                pl.semaphore_signal(barrier, inc=1, device_id=at(y, there, i % 2), device_id_type=MESH)

            return carry

        lax.fori_loop(0, 2 * n_z, greet, 0)
        for step in range(1, n_y):
            pl.semaphore_signal(barrier, inc=1, device_id=at((y + step) % n_y, gz, 0), device_id_type=MESH)

    @pl.when(jnp.logical_not(is_root))
    def _():
        parent_z = by_index({key: node[0] for key, node in parent.items() if node[0] != key[0]}, -1)
        parent_z = jnp.where(parent_z < 0, gz, parent_z)
        parent_slot = by_index({key: node[1] for key, node in parent.items()}, 0)
        pl.semaphore_signal(barrier, inc=1, device_id=at(y, parent_z, parent_slot), device_id_type=MESH)

    copies[0].wait()
    y_high, y_low = blocks(ty[...])
    y_both = jnp.concatenate([y_high, y_low], axis=0).astype(BF16)
    copies[3].wait()
    copies[4].wait()
    x_high = dot_0(tx[0], pick[...]).astype(BF16)
    x_low = dot_0(tx[1], pick[...]).astype(BF16)
    copies[1].wait()
    copies[2].wait()
    along = along_y(st[...].reshape(512, 256), y_both, y_high.astype(BF16))
    for copy in copies[5:]:
        copy.wait()
    partial = along_x(along, x_high, x_low)
    held = folded(jnp.concatenate([er[0], er[1]], axis=0), fold[...], rows[16:24], rows[24:32])
    row = lax.broadcasted_iota(jnp.int32, (8, LANES), 0)
    me = gx * n_z + gz
    keeper = jnp.where(row < 4, owner[0, 0], owner[0, 1])
    share = jnp.where(keeper == me, held, 0.0) - rows[0:8] * partial
    for c in range(CHUNKS):
        pay[c] = share[:, c * 128 : (c + 1) * 128]

    def prepare():
        rate = jnp.zeros((8, LANES), F32)
        limit = jnp.zeros((8, LANES), jnp.int32)
        for f in range(8):
            rate = jnp.where(row == f, relax[f // 4, f % 4], rate)
            limit = jnp.where(row == f, cutoff[f // 4, f % 4], limit)
        scale[...] = jnp.where(rows[8:16] <= (limit * limit).astype(F32), rate, 0.0)
        for part in range(2):
            tx_wide[part] = dot_0(pick[...], tx[part]).astype(BF16)
        by[...] = back_y_tables(y_high, y_low)

    n_far = 2 * (FAR[1] - FAR[0])
    n_near = 2 * n_z - 1 - n_far

    def remote(src, dst, which, target):
        return pltpu.make_async_remote_copy(
            src, dst, send_sem.at[which % 3], recv_sem.at[which], device_id=target, device_id_type=MESH
        )

    root = at(y, 16, 0)
    n_children = by_index({key: len(nodes) for key, nodes in children.items()}, 0)
    busy = [key for key, nodes in children.items() if key == (0, 1) or len(nodes) > 1]
    top = [(r, 0) for r in ROOTS]
    is_relay = jnp.logical_and(slot == 0, n_children == 1)

    def pass_on(key):
        for z, child_slot in children[key]:
            remote(total, total, 2, at(y, z, child_slot)).start()

    pl.semaphore_wait(barrier, n_children + jnp.where(is_root, len(ROOTS) + n_y - 2, len(ROOTS)))
    for r in ROOTS:
        from_root = (index + 2 * n_z - 2 * r) % (2 * n_z)
        far = jnp.logical_and(from_root >= 2 * FAR[0], from_root < 2 * FAR[1])
        after = jnp.where(from_root >= 2 * FAR[1], from_root - n_far, from_root) - 1
        place = jnp.where(far, n_near + from_root - 2 * FAR[0], after)

        @pl.when(index != 2 * r)
        def _():
            pltpu.make_async_remote_copy(
                pay, got.at[place], send_sem.at[0], recv_sem.at[jnp.where(far, 3, 0)],
                device_id=at(y, r, 0), device_id_type=MESH,
            ).start()

    prepare()

    @pl.when(jnp.logical_not(is_root))
    def _():
        remote(total, total, 2, root).wait_recv()

    @pl.when(is_root)
    def _():
        near, far = got.at[pl.ds(0, n_near)], got.at[pl.ds(n_near, n_far)]
        remote(near, near, 0, root).wait_recv()
        first = pay[...] + jnp.sum(near[...], axis=0)
        remote(far, far, 3, root).wait_recv()
        mine_y[...] = first + jnp.sum(far[...], axis=0)
        for step in sorted(range(1, n_y), key=lambda step: -min(step, n_y - step)):
            remote(mine_y, got_y.at[step - 1], 1, at((y + step) % n_y, gz, 0)).start()
        remote(got_y, got_y, 1, root).wait_recv()
        total[...] = mine_y[...] + jnp.sum(got_y[...], axis=0)

    for key in top + [key for key in busy if key not in top]:
        pl.when(index == 2 * key[0] + key[1])(functools.partial(pass_on, key))

    @pl.when(is_relay)
    def _():
        remote(total, total, 2, at(y, gz, 1)).start()

    summed = jnp.concatenate([total[c] for c in range(CHUNKS)], axis=1)
    added = back_y(back_x(summed * scale[...], tx_wide[...]), by[...])
    for h in range(2):
        block = added[256 * h : 256 * (h + 1)].reshape(4, 64, 256)
        out[h] = st[4 * h : 4 * h + 4] + block

    def pass_on_sent(count):
        sent = got.at[pl.ds(0, count)]
        remote(sent, sent, 2, root).wait_send()

    def shares_sent(count):
        sent = got.at[pl.ds(0, count)]
        remote(sent, sent, 0, root).wait_send()

    @pl.when(is_root)
    def _():
        remote(got_y, got_y, 1, root).wait_send()
        shares_sent(len(ROOTS) - 1)

    @pl.when(jnp.logical_not(is_root))
    def _():
        shares_sent(len(ROOTS))

    for key in busy:
        pl.when(index == 2 * key[0] + key[1])(functools.partial(pass_on_sent, len(children[key])))

    @pl.when(is_relay)
    def _():
        pass_on_sent(1)


def solution(mesh):
    n_gx, n_gy = mesh.shape["gx"], mesh.shape["gy"]
    tables = (along_y_tables(n_gy, FIELDS // 2), along_x_tables(n_gx), pick_table(), *fold_tables())

    def body(model_state, cutoff, relax_rate, owner_map, era_store):
        arrays = (cutoff, relax_rate, owner_map, model_state, era_store, *(jnp.asarray(t) for t in tables))
        vmem = pltpu.VMEM
        return pl.pallas_call(
            functools.partial(kernel, n_gx // 2, n_gy),
            out_shape=jax.ShapeDtypeStruct(model_state.shape, F32),
            in_specs=[pl.BlockSpec(memory_space=pltpu.HBM)] * 10,
            out_specs=pl.BlockSpec(memory_space=vmem),
            scratch_shapes=[
                pltpu.SMEM((2, 4), jnp.int32),
                pltpu.SMEM((2, 4), F32),
                pltpu.SMEM((1, 2), jnp.int32),
                vmem((8, 64, 256), F32),
                vmem((2, 4, 2 * NK * NK), F32),
                vmem((2, PAD, 256), BF16),
                vmem((2, WIDE, 256), BF16),
                vmem((WIDE, LANES), BF16),
                vmem((NK * NK, LANES), BF16),
                vmem((4 * FIELDS, LANES), F32),
                vmem((512, 512), BF16),
                vmem((2, LANES, 256), BF16),
                vmem((8, LANES), F32),
                vmem((CHUNKS, 8, 128), F32),
                vmem((2 * n_gy - 1, CHUNKS, 8, 128), F32),
                vmem((n_gx // 2 - 1, CHUNKS, 8, 128), F32),
                vmem((CHUNKS, 8, 128), F32),
                vmem((CHUNKS, 8, 128), F32),
                pltpu.SemaphoreType.DMA((11,)),
                pltpu.SemaphoreType.DMA((3,)),
                pltpu.SemaphoreType.DMA((4,)),
            ],
            compiler_params=pltpu.CompilerParams(
                collective_id=0, has_side_effects=True, vmem_limit_bytes=16 << 20
            ),
        )(*(pltpu.with_memory_space_constraint(array, pltpu.HBM) for array in arrays))

    placed = (
        P(None, "lev", "gy", "gx"),
        P(None, "lev"),
        P(None, "lev"),
        P("lev", None),
        P(("gx", "gy"), None, "lev", None),
    )
    return jax.shard_map(
        body, mesh=mesh, in_specs=placed, out_specs=P(None, "lev", "gy", "gx"), check_vma=False
    )
```

```python
import functools

import jax
import jax.numpy as jnp
import ml_dtypes
import numpy as np
from jax import lax
from jax.experimental import pallas as pl
from jax.experimental.pallas import tpu as pltpu
from jax.sharding import PartitionSpec as P

NX = 2048
NY = 2048
KC = 10
NK = 21
PAD = 24
WIDE = 32
FIELDS = 8
ROWS = NK * FIELDS
LANES = 512
CHUNKS = LANES // 128
ROOTS = (0, 8)
FAR = (12, 20)
MESH = pl.DeviceIdType.MESH
BF16 = jnp.bfloat16
F32 = jnp.float32


def split(table):
    high = table.astype(ml_dtypes.bfloat16)
    low = (table - high.astype(np.float64)).astype(ml_dtypes.bfloat16)
    return np.stack([high, low])


def wavenumbers():
    return np.concatenate([np.arange(KC + 1), np.arange(1, KC + 1)])


def basis(length):
    wave = wavenumbers()
    angle = 2.0 * np.pi * np.mod(wave[:, None] * np.arange(length)[None, :], length) / length
    is_cos = (np.arange(NK) <= KC)[:, None]
    return np.where(is_cos, np.cos(angle), np.sin(angle))


def along_y_tables(n_gy, fields):
    ny = NY // n_gy
    out = np.zeros((n_gy, PAD, fields * ny))
    out[:, :NK] = np.tile(basis(NY).reshape(NK, n_gy, ny).transpose(1, 0, 2), (1, 1, fields))
    high, low = split(out)
    return np.stack([high, low], axis=1)


def along_x_tables(n_gx):
    nx = NX // n_gx
    out = np.zeros((n_gx, WIDE, nx))
    out[:, :NK] = basis(NX).reshape(NK, n_gx, nx).transpose(1, 0, 2)
    high, low = split(out)
    return np.stack([high, low], axis=1)


def pick_table():
    out = np.zeros((WIDE, LANES))
    p = np.arange(NK * NK)
    out[p % NK, p] = 1.0
    return out.astype(ml_dtypes.bfloat16)


def fold_tables():
    wave = np.arange(NK) - KC
    number = wavenumbers()
    is_cos = np.arange(NK) <= KC
    hit = (number[:, None] == np.abs(wave)[None, :]).astype(np.float64)
    factor = np.where(is_cos[:, None], hit, hit * np.sign(wave)[None, :])
    table = np.zeros((NK * NK, LANES))
    table[:, : NK * NK] = np.einsum("ak,bj->kjab", factor, factor).reshape(NK * NK, NK * NK)
    both_cos = np.outer(is_cos, is_cos)
    both_sin = np.outer(~is_cos, ~is_cos)
    twice = np.where(number == 0, 1.0, 2.0)
    kinds = [
        np.outer(twice, twice) / (NX * NY),
        number[:, None] ** 2 + number[None, :] ** 2,
        both_cos.astype(np.float64) - both_sin.astype(np.float64),
        -(~(both_cos | both_sin)).astype(np.float64),
    ]
    rows = np.zeros((4, FIELDS, LANES), np.float32)
    for kind, value in enumerate(kinds):
        rows[kind, :, : NK * NK] = value.reshape(-1)
    return table.astype(ml_dtypes.bfloat16), rows.reshape(4 * FIELDS, LANES)


def halves(value):
    high = value.astype(BF16)
    low = (value - high.astype(F32)).astype(BF16)
    return high, low


def dot(left, right):
    return lax.dot_general(left, right, (((1,), (0,)), ((), ())), preferred_element_type=F32)


def dot_t(left, right):
    return lax.dot_general(left, right, (((1,), (1,)), ((), ())), preferred_element_type=F32)


def blocks(table):
    shape = (FIELDS, 2 * table.shape[2])
    field = lax.broadcasted_iota(jnp.int32, shape, 0)
    lane = lax.broadcasted_iota(jnp.int32, shape, 1)
    width = shape[1] // FIELDS
    keep = (lane >= field * width) & (lane < (field + 1) * width)
    out = []
    for part in range(2):
        half = table[part].astype(F32)
        whole = jnp.concatenate([half, half], axis=1)[:NK]
        out.append(jnp.where(keep[None], whole[:, None, :], 0.0).reshape(ROWS, shape[1]))
    return out


def dot_0(left, right):
    return lax.dot_general(left, right, (((0,), (0,)), ((), ())), preferred_element_type=F32)


def along_y(block, both_tables, high_table):
    high, low = halves(block)
    both = dot(both_tables, high)
    return both[:ROWS] + both[ROWS:] + dot(high_table, low)


def spans(a):
    return [
        (t, max(a * NK - 128 * t, 0), min((a + 1) * NK - 128 * t, 128))
        for t in range(a * NK // 128, (a * NK + NK - 1) // 128 + 1)
    ]


def along_x(value, table, pick):
    high, low = halves(value)
    narrow = dot_t(high, table[0]) + dot_t(high, table[1]) + dot_t(low, table[0])
    high, low = halves(narrow)
    wide = dot(high, pick) + dot(low, pick)
    lane = lax.broadcasted_iota(jnp.int32, (FIELDS, 128), 1)
    tiles = [None] * CHUNKS
    for a in range(NK):
        for t, start, _ in spans(a):
            here = wide[a * FIELDS : (a + 1) * FIELDS, t * 128 : (t + 1) * 128]
            tiles[t] = here if tiles[t] is None else jnp.where(lane >= start, here, tiles[t])
    return jnp.concatenate(tiles, axis=1)


def folded(era, table, sign_re, sign_im):
    parts = []
    for part in range(2):
        value = era[:, part * NK * NK : (part + 1) * NK * NK]
        first = value.astype(BF16).astype(F32)
        rest = value - first
        second = rest.astype(BF16).astype(F32)
        parts += [first, second, rest - second]
    out = dot(jnp.concatenate(parts, axis=0).astype(BF16), table)
    real = out[0:8] + out[8:16] + out[16:24]
    imag = out[24:32] + out[32:40] + out[40:48]
    return sign_re * real + sign_im * imag


def spread(coefs):
    lane = lax.broadcasted_iota(jnp.int32, (FIELDS, 128), 1)
    zero = jnp.zeros((FIELDS, 128), F32)
    rows = []
    for a in range(NK):
        tiles = [zero] * CHUNKS
        for t, start, stop in spans(a):
            tiles[t] = jnp.where((lane >= start) & (lane < stop), coefs[:, t * 128 : (t + 1) * 128], 0.0)
        rows.append(jnp.concatenate(tiles, axis=1))
    return jnp.concatenate(rows, axis=0)


def back_x(coefs, table):
    first = coefs.astype(BF16).astype(F32)
    high = spread(first)
    both = dot(jnp.concatenate([high, spread(coefs - first)], axis=0).astype(BF16), table[0])
    return both[:ROWS] + both[ROWS:] + dot(high.astype(BF16), table[1])


def back_y_tables(high, low):
    fill = jnp.zeros((512 - 3 * ROWS, high.shape[1]), F32)
    return jnp.concatenate([high, low, high, fill], axis=0).T.astype(BF16)


def back_y(value, table):
    high = value.astype(BF16).astype(F32)
    fill = jnp.zeros((512 - 3 * ROWS, value.shape[1]), F32)
    return dot(table, jnp.concatenate([high, high, value - high, fill], axis=0).astype(BF16))


def way_back():
    children = {
        (0, 0): [(1, 1), (1, 0), (2, 1), (2, 0), (0, 1), (3, 1), (4, 0), (3, 0)],
        (0, 1): [(23, 0), (31, 0)],
        (8, 0): [(4, 1), (5, 1), (5, 0), (6, 0), (6, 1), (7, 0), (12, 0), (8, 1), (9, 0), (10, 0), (11, 0)],
        (12, 0): [(12, 1), (13, 0), (14, 0), (15, 0)],
        (19, 0): [(16, 0), (17, 0), (18, 0), (19, 1)],
        (23, 0): [(19, 0), (20, 0), (21, 0), (22, 0), (23, 1)],
        (31, 0): [(31, 1)] + [(z, 0) for z in range(24, 31)],
    }
    parent = {child: node for node, nodes in children.items() for child in nodes}
    for z in range(1, 32):
        if (z, 1) not in parent:
            parent[z, 1] = (z, 0)
            children[z, 0] = [(z, 1)]
    return children, parent


def kernel(
    n_y, n_z,
    cutoff_in, relax_in, owner_in, state, era, tab_y, tab_x, tab_pick, tab_fold, tab_rows,
    out,
    cutoff, relax, owner, st, er, ty, tx, pick, fold, rows, by, tx_wide, scale, pay, got, got_y, mine_y, total,
    in_sem, send_sem, recv_sem,
):
    gx = lax.axis_index("gx")
    gz = lax.axis_index("gy")
    lev = lax.axis_index("lev")
    y = gx // 2
    children, parent = way_back()

    def swapped(y_pos):
        return jnp.where(jnp.logical_and(y_pos == 0, lev == 0), 1, 0)

    def at(y_pos, z_pos, slot):
        flip = swapped(y_pos)
        other = slot + flip - 2 * slot * flip
        return {"gx": y_pos * 2 + jnp.where(z_pos == 0, other, slot), "gy": z_pos}

    flip = swapped(y)
    core = gx % 2
    slot = jnp.where(gz == 0, core + flip - 2 * core * flip, core)
    index = 2 * gz + slot
    is_root = functools.reduce(jnp.logical_or, [index == 2 * r for r in ROOTS])

    def by_index(table, default):
        value = jnp.int32(default)
        for key, entry in table.items():
            if entry != default:
                value = jnp.where(index == 2 * key[0] + key[1], entry, value)
        return value

    copies = [
        pltpu.make_async_copy(tab_y.at[gz], ty, in_sem.at[0]),
        pltpu.make_async_copy(state.at[0], st.at[pl.ds(0, 4)], in_sem.at[1]),
        pltpu.make_async_copy(state.at[1], st.at[pl.ds(4, 4)], in_sem.at[2]),
        pltpu.make_async_copy(tab_x.at[gx], tx, in_sem.at[3]),
        pltpu.make_async_copy(tab_pick, pick, in_sem.at[4]),
        pltpu.make_async_copy(era.at[0], er, in_sem.at[5]),
        pltpu.make_async_copy(tab_fold, fold, in_sem.at[6]),
        pltpu.make_async_copy(tab_rows, rows, in_sem.at[7]),
        pltpu.make_async_copy(owner_in, owner, in_sem.at[8]),
        pltpu.make_async_copy(cutoff_in, cutoff, in_sem.at[9]),
        pltpu.make_async_copy(relax_in, relax, in_sem.at[10]),
    ]
    for copy in copies:
        copy.start()

    barrier = pltpu.get_barrier_semaphore()

    @pl.when(is_root)
    def _():
        def greet(i, carry):
            there = (gz + n_z // 4 + i // 2) % n_z

            @pl.when(2 * there + i % 2 != index)
            def _():
                pl.semaphore_signal(barrier, inc=1, device_id=at(y, there, i % 2), device_id_type=MESH)

            return carry

        lax.fori_loop(0, 2 * n_z, greet, 0)
        for step in range(1, n_y):
            pl.semaphore_signal(barrier, inc=1, device_id=at((y + step) % n_y, gz, 0), device_id_type=MESH)

    @pl.when(jnp.logical_not(is_root))
    def _():
        parent_z = by_index({key: node[0] for key, node in parent.items() if node[0] != key[0]}, -1)
        parent_z = jnp.where(parent_z < 0, gz, parent_z)
        parent_slot = by_index({key: node[1] for key, node in parent.items()}, 0)
        pl.semaphore_signal(barrier, inc=1, device_id=at(y, parent_z, parent_slot), device_id_type=MESH)

    copies[0].wait()
    y_high, y_low = blocks(ty[...])
    y_both = jnp.concatenate([y_high, y_low], axis=0).astype(BF16)
    copies[1].wait()
    copies[2].wait()
    along = along_y(st[...].reshape(512, 256), y_both, y_high.astype(BF16))
    for copy in copies[3:]:
        copy.wait()
    partial = along_x(along, tx[...], pick[...])
    held = folded(jnp.concatenate([er[0], er[1]], axis=0), fold[...], rows[16:24], rows[24:32])
    row = lax.broadcasted_iota(jnp.int32, (8, LANES), 0)
    me = gx * n_z + gz
    keeper = jnp.where(row < 4, owner[0, 0], owner[0, 1])
    share = jnp.where(keeper == me, held, 0.0) - rows[0:8] * partial
    for c in range(CHUNKS):
        pay[c] = share[:, c * 128 : (c + 1) * 128]

    def prepare():
        rate = jnp.zeros((8, LANES), F32)
        limit = jnp.zeros((8, LANES), jnp.int32)
        for f in range(8):
            rate = jnp.where(row == f, relax[f // 4, f % 4], rate)
            limit = jnp.where(row == f, cutoff[f // 4, f % 4], limit)
        scale[...] = jnp.where(rows[8:16] <= (limit * limit).astype(F32), rate, 0.0)
        for part in range(2):
            tx_wide[part] = dot_0(pick[...], tx[part]).astype(BF16)
        by[...] = back_y_tables(y_high, y_low)

    n_far = 2 * (FAR[1] - FAR[0])
    n_near = 2 * n_z - 1 - n_far

    def remote(src, dst, which, target):
        return pltpu.make_async_remote_copy(
            src, dst, send_sem.at[which % 3], recv_sem.at[which], device_id=target, device_id_type=MESH
        )

    root = at(y, 16, 0)
    n_children = by_index({key: len(nodes) for key, nodes in children.items()}, 0)
    busy = [key for key, nodes in children.items() if key == (0, 1) or len(nodes) > 1]
    top = [(r, 0) for r in ROOTS]
    is_relay = jnp.logical_and(slot == 0, n_children == 1)

    def pass_on(key):
        for z, child_slot in children[key]:
            remote(total, total, 2, at(y, z, child_slot)).start()

    pl.semaphore_wait(barrier, n_children + jnp.where(is_root, len(ROOTS) + n_y - 2, len(ROOTS)))
    for r in ROOTS:
        from_root = (index + 2 * n_z - 2 * r) % (2 * n_z)
        far = jnp.logical_and(from_root >= 2 * FAR[0], from_root < 2 * FAR[1])
        after = jnp.where(from_root >= 2 * FAR[1], from_root - n_far, from_root) - 1
        place = jnp.where(far, n_near + from_root - 2 * FAR[0], after)

        @pl.when(index != 2 * r)
        def _():
            pltpu.make_async_remote_copy(
                pay, got.at[place], send_sem.at[0], recv_sem.at[jnp.where(far, 3, 0)],
                device_id=at(y, r, 0), device_id_type=MESH,
            ).start()

    prepare()

    @pl.when(jnp.logical_not(is_root))
    def _():
        remote(total, total, 2, root).wait_recv()

    @pl.when(is_root)
    def _():
        near, far = got.at[pl.ds(0, n_near)], got.at[pl.ds(n_near, n_far)]
        remote(near, near, 0, root).wait_recv()
        first = pay[...] + jnp.sum(near[...], axis=0)
        remote(far, far, 3, root).wait_recv()
        mine_y[...] = first + jnp.sum(far[...], axis=0)
        for step in sorted(range(1, n_y), key=lambda step: -min(step, n_y - step)):
            remote(mine_y, got_y.at[step - 1], 1, at((y + step) % n_y, gz, 0)).start()
        remote(got_y, got_y, 1, root).wait_recv()
        total[...] = mine_y[...] + jnp.sum(got_y[...], axis=0)

    for key in top + [key for key in busy if key not in top]:
        pl.when(index == 2 * key[0] + key[1])(functools.partial(pass_on, key))

    @pl.when(is_relay)
    def _():
        remote(total, total, 2, at(y, gz, 1)).start()

    summed = jnp.concatenate([total[c] for c in range(CHUNKS)], axis=1)
    added = back_y(back_x(summed * scale[...], tx_wide[...]), by[...])
    for h in range(2):
        block = added[256 * h : 256 * (h + 1)].reshape(4, 64, 256)
        out[h] = st[4 * h : 4 * h + 4] + block

    def pass_on_sent(count):
        sent = got.at[pl.ds(0, count)]
        remote(sent, sent, 2, root).wait_send()

    def shares_sent(count):
        sent = got.at[pl.ds(0, count)]
        remote(sent, sent, 0, root).wait_send()

    @pl.when(is_root)
    def _():
        remote(got_y, got_y, 1, root).wait_send()
        shares_sent(len(ROOTS) - 1)

    @pl.when(jnp.logical_not(is_root))
    def _():
        shares_sent(len(ROOTS))

    for key in busy:
        pl.when(index == 2 * key[0] + key[1])(functools.partial(pass_on_sent, len(children[key])))

    @pl.when(is_relay)
    def _():
        pass_on_sent(1)


def solution(mesh):
    n_gx, n_gy = mesh.shape["gx"], mesh.shape["gy"]
    tables = (along_y_tables(n_gy, FIELDS // 2), along_x_tables(n_gx), pick_table(), *fold_tables())

    def body(model_state, cutoff, relax_rate, owner_map, era_store):
        arrays = (cutoff, relax_rate, owner_map, model_state, era_store, *(jnp.asarray(t) for t in tables))
        vmem = pltpu.VMEM
        return pl.pallas_call(
            functools.partial(kernel, n_gx // 2, n_gy),
            out_shape=jax.ShapeDtypeStruct(model_state.shape, F32),
            in_specs=[pl.BlockSpec(memory_space=pltpu.HBM)] * 10,
            out_specs=pl.BlockSpec(memory_space=vmem),
            scratch_shapes=[
                pltpu.SMEM((2, 4), jnp.int32),
                pltpu.SMEM((2, 4), F32),
                pltpu.SMEM((1, 2), jnp.int32),
                vmem((8, 64, 256), F32),
                vmem((2, 4, 2 * NK * NK), F32),
                vmem((2, PAD, 256), BF16),
                vmem((2, WIDE, 256), BF16),
                vmem((WIDE, LANES), BF16),
                vmem((NK * NK, LANES), BF16),
                vmem((4 * FIELDS, LANES), F32),
                vmem((512, 512), BF16),
                vmem((2, LANES, 256), BF16),
                vmem((8, LANES), F32),
                vmem((CHUNKS, 8, 128), F32),
                vmem((2 * n_gy - 1, CHUNKS, 8, 128), F32),
                vmem((n_gx // 2 - 1, CHUNKS, 8, 128), F32),
                vmem((CHUNKS, 8, 128), F32),
                vmem((CHUNKS, 8, 128), F32),
                pltpu.SemaphoreType.DMA((11,)),
                pltpu.SemaphoreType.DMA((3,)),
                pltpu.SemaphoreType.DMA((4,)),
            ],
            compiler_params=pltpu.CompilerParams(
                collective_id=0, has_side_effects=True, vmem_limit_bytes=16 << 20
            ),
        )(*(pltpu.with_memory_space_constraint(array, pltpu.HBM) for array in arrays))

    placed = (
        P(None, "lev", "gy", "gx"),
        P(None, "lev"),
        P(None, "lev"),
        P("lev", None),
        P(("gx", "gy"), None, "lev", None),
    )
    return jax.shard_map(
        body, mesh=mesh, in_specs=placed, out_specs=P(None, "lev", "gy", "gx"), check_vma=False
    )
```

```python
import functools

import jax
import jax.numpy as jnp
import ml_dtypes
import numpy as np
from jax import lax
from jax.experimental import pallas as pl
from jax.experimental.pallas import tpu as pltpu
from jax.sharding import PartitionSpec as P

NX = 2048
NY = 2048
KC = 10
NK = 21
PAD = 24
WIDE = 32
FIELDS = 8
ROWS = NK * FIELDS
LANES = 512
CHUNKS = LANES // 128
ROOTS = (0, 8)
FAR = (12, 20)
MESH = pl.DeviceIdType.MESH
BF16 = jnp.bfloat16
F32 = jnp.float32


def split(table):
    high = table.astype(ml_dtypes.bfloat16)
    low = (table - high.astype(np.float64)).astype(ml_dtypes.bfloat16)
    return np.stack([high, low])


def wavenumbers():
    return np.concatenate([np.arange(KC + 1), np.arange(1, KC + 1)])


def basis(length):
    wave = wavenumbers()
    angle = 2.0 * np.pi * np.mod(wave[:, None] * np.arange(length)[None, :], length) / length
    is_cos = (np.arange(NK) <= KC)[:, None]
    return np.where(is_cos, np.cos(angle), np.sin(angle))


def along_y_tables(n_gy, fields):
    ny = NY // n_gy
    out = np.zeros((n_gy, PAD, fields * ny))
    out[:, :NK] = np.tile(basis(NY).reshape(NK, n_gy, ny).transpose(1, 0, 2), (1, 1, fields))
    high, low = split(out)
    return np.stack([high, low], axis=1)


def along_x_tables(n_gx):
    nx = NX // n_gx
    out = np.zeros((n_gx, WIDE, nx))
    out[:, :NK] = basis(NX).reshape(NK, n_gx, nx).transpose(1, 0, 2)
    high, low = split(out)
    return np.stack([high, low], axis=1)


def pick_table():
    out = np.zeros((WIDE, LANES))
    p = np.arange(NK * NK)
    out[p % NK, p] = 1.0
    return out.astype(ml_dtypes.bfloat16)


def fold_tables():
    wave = np.arange(NK) - KC
    number = wavenumbers()
    is_cos = np.arange(NK) <= KC
    hit = (number[:, None] == np.abs(wave)[None, :]).astype(np.float64)
    factor = np.where(is_cos[:, None], hit, hit * np.sign(wave)[None, :])
    table = np.zeros((NK * NK, LANES))
    table[:, : NK * NK] = np.einsum("ak,bj->kjab", factor, factor).reshape(NK * NK, NK * NK)
    both_cos = np.outer(is_cos, is_cos)
    both_sin = np.outer(~is_cos, ~is_cos)
    twice = np.where(number == 0, 1.0, 2.0)
    kinds = [
        np.outer(twice, twice) / (NX * NY),
        number[:, None] ** 2 + number[None, :] ** 2,
        both_cos.astype(np.float64) - both_sin.astype(np.float64),
        -(~(both_cos | both_sin)).astype(np.float64),
    ]
    rows = np.zeros((4, FIELDS, LANES), np.float32)
    for kind, value in enumerate(kinds):
        rows[kind, :, : NK * NK] = value.reshape(-1)
    return table.astype(ml_dtypes.bfloat16), rows.reshape(4 * FIELDS, LANES)


def halves(value):
    high = value.astype(BF16)
    low = (value - high.astype(F32)).astype(BF16)
    return high, low


def dot(left, right):
    return lax.dot_general(left, right, (((1,), (0,)), ((), ())), preferred_element_type=F32)


def dot_t(left, right):
    return lax.dot_general(left, right, (((1,), (1,)), ((), ())), preferred_element_type=F32)


def blocks(table):
    shape = (FIELDS, 2 * table.shape[2])
    field = lax.broadcasted_iota(jnp.int32, shape, 0)
    lane = lax.broadcasted_iota(jnp.int32, shape, 1)
    width = shape[1] // FIELDS
    keep = (lane >= field * width) & (lane < (field + 1) * width)
    out = []
    for part in range(2):
        half = table[part].astype(F32)
        whole = jnp.concatenate([half, half], axis=1)[:NK]
        out.append(jnp.where(keep[None], whole[:, None, :], 0.0).reshape(ROWS, shape[1]))
    return out


def dot_0(left, right):
    return lax.dot_general(left, right, (((0,), (0,)), ((), ())), preferred_element_type=F32)


def along_y(block, both_tables, high_table):
    high, low = halves(block)
    both = dot(both_tables, high)
    return both[:ROWS] + both[ROWS:] + dot(high_table, low)


def spans(a):
    return [
        (t, max(a * NK - 128 * t, 0), min((a + 1) * NK - 128 * t, 128))
        for t in range(a * NK // 128, (a * NK + NK - 1) // 128 + 1)
    ]


def along_x(value, high_table, low_table):
    high, low = halves(value)
    wide = dot(high, high_table) + dot(high, low_table) + dot(low, high_table)
    lane = lax.broadcasted_iota(jnp.int32, (FIELDS, 128), 1)
    tiles = [None] * CHUNKS
    for a in range(NK):
        for t, start, _ in spans(a):
            here = wide[a * FIELDS : (a + 1) * FIELDS, t * 128 : (t + 1) * 128]
            tiles[t] = here if tiles[t] is None else jnp.where(lane >= start, here, tiles[t])
    return jnp.concatenate(tiles, axis=1)


def folded(era, table, sign_re, sign_im):
    parts = []
    for part in range(2):
        value = era[:, part * NK * NK : (part + 1) * NK * NK]
        first = value.astype(BF16).astype(F32)
        rest = value - first
        second = rest.astype(BF16).astype(F32)
        parts += [first, second, rest - second]
    out = dot(jnp.concatenate(parts, axis=0).astype(BF16), table)
    real = out[0:8] + out[8:16] + out[16:24]
    imag = out[24:32] + out[32:40] + out[40:48]
    return sign_re * real + sign_im * imag


def spread(coefs):
    lane = lax.broadcasted_iota(jnp.int32, (FIELDS, 128), 1)
    zero = jnp.zeros((FIELDS, 128), F32)
    rows = []
    for a in range(NK):
        tiles = [zero] * CHUNKS
        for t, start, stop in spans(a):
            tiles[t] = jnp.where((lane >= start) & (lane < stop), coefs[:, t * 128 : (t + 1) * 128], 0.0)
        rows.append(jnp.concatenate(tiles, axis=1))
    return jnp.concatenate(rows, axis=0)


def back_x(coefs, table):
    first = coefs.astype(BF16).astype(F32)
    high = spread(first)
    both = dot(jnp.concatenate([high, spread(coefs - first)], axis=0).astype(BF16), table[0])
    return both[:ROWS] + both[ROWS:] + dot(high.astype(BF16), table[1])


def back_y_tables(high, low):
    fill = jnp.zeros((512 - 3 * ROWS, high.shape[1]), F32)
    return jnp.concatenate([high, low, high, fill], axis=0).T.astype(BF16)


def back_y(value, table):
    high = value.astype(BF16).astype(F32)
    fill = jnp.zeros((512 - 3 * ROWS, value.shape[1]), F32)
    return dot(table, jnp.concatenate([high, high, value - high, fill], axis=0).astype(BF16))


def way_back():
    children = {
        (0, 0): [(1, 1), (1, 0), (2, 1), (2, 0), (0, 1), (3, 1), (4, 0), (3, 0)],
        (0, 1): [(23, 0), (31, 0)],
        (8, 0): [(4, 1), (5, 1), (5, 0), (6, 0), (6, 1), (7, 0), (12, 0), (8, 1), (9, 0), (10, 0), (11, 0)],
        (12, 0): [(12, 1), (13, 0), (14, 0), (15, 0)],
        (19, 0): [(16, 0), (17, 0), (18, 0), (19, 1)],
        (23, 0): [(19, 0), (20, 0), (21, 0), (22, 0), (23, 1)],
        (31, 0): [(31, 1)] + [(z, 0) for z in range(24, 31)],
    }
    parent = {child: node for node, nodes in children.items() for child in nodes}
    for z in range(1, 32):
        if (z, 1) not in parent:
            parent[z, 1] = (z, 0)
            children[z, 0] = [(z, 1)]
    return children, parent


def kernel(
    n_y, n_z,
    cutoff_in, relax_in, owner_in, state, era, tab_y, tab_x, tab_pick, tab_fold, tab_rows,
    out,
    cutoff, relax, owner, st, er, ty, tx, pick, fold, rows, by, tx_wide, scale, pay, got, got_y, mine_y, total,
    in_sem, send_sem, recv_sem,
):
    gx = lax.axis_index("gx")
    gz = lax.axis_index("gy")
    lev = lax.axis_index("lev")
    y = gx // 2
    children, parent = way_back()

    def swapped(y_pos):
        return jnp.where(jnp.logical_and(y_pos == 0, lev == 0), 1, 0)

    def at(y_pos, z_pos, slot):
        flip = swapped(y_pos)
        other = slot + flip - 2 * slot * flip
        return {"gx": y_pos * 2 + jnp.where(z_pos == 0, other, slot), "gy": z_pos}

    flip = swapped(y)
    core = gx % 2
    slot = jnp.where(gz == 0, core + flip - 2 * core * flip, core)
    index = 2 * gz + slot
    is_root = functools.reduce(jnp.logical_or, [index == 2 * r for r in ROOTS])

    def by_index(table, default):
        value = jnp.int32(default)
        for key, entry in table.items():
            if entry != default:
                value = jnp.where(index == 2 * key[0] + key[1], entry, value)
        return value

    copies = [
        pltpu.make_async_copy(tab_y.at[gz], ty, in_sem.at[0]),
        pltpu.make_async_copy(state.at[0], st.at[pl.ds(0, 4)], in_sem.at[1]),
        pltpu.make_async_copy(state.at[1], st.at[pl.ds(4, 4)], in_sem.at[2]),
        pltpu.make_async_copy(tab_x.at[gx], tx, in_sem.at[3]),
        pltpu.make_async_copy(tab_pick, pick, in_sem.at[4]),
        pltpu.make_async_copy(era.at[0], er, in_sem.at[5]),
        pltpu.make_async_copy(tab_fold, fold, in_sem.at[6]),
        pltpu.make_async_copy(tab_rows, rows, in_sem.at[7]),
        pltpu.make_async_copy(owner_in, owner, in_sem.at[8]),
        pltpu.make_async_copy(cutoff_in, cutoff, in_sem.at[9]),
        pltpu.make_async_copy(relax_in, relax, in_sem.at[10]),
    ]
    for copy in [copies[i] for i in (0, 3, 4, 1, 2, 5, 6, 7, 8, 9, 10)]:
        copy.start()

    barrier = pltpu.get_barrier_semaphore()

    @pl.when(is_root)
    def _():
        def greet(i, carry):
            there = (gz + n_z // 4 + i // 2) % n_z

            @pl.when(2 * there + i % 2 != index)
            def _():
                pl.semaphore_signal(barrier, inc=1, device_id=at(y, there, i % 2), device_id_type=MESH)

            return carry

        lax.fori_loop(0, 2 * n_z, greet, 0)
        for step in range(1, n_y):
            pl.semaphore_signal(barrier, inc=1, device_id=at((y + step) % n_y, gz, 0), device_id_type=MESH)

    @pl.when(jnp.logical_not(is_root))
    def _():
        parent_z = by_index({key: node[0] for key, node in parent.items() if node[0] != key[0]}, -1)
        parent_z = jnp.where(parent_z < 0, gz, parent_z)
        parent_slot = by_index({key: node[1] for key, node in parent.items()}, 0)
        pl.semaphore_signal(barrier, inc=1, device_id=at(y, parent_z, parent_slot), device_id_type=MESH)

    copies[0].wait()
    y_high, y_low = blocks(ty[...])
    y_both = jnp.concatenate([y_high, y_low], axis=0).astype(BF16)
    copies[3].wait()
    copies[4].wait()
    x_high = dot_0(tx[0], pick[...]).astype(BF16)
    x_low = dot_0(tx[1], pick[...]).astype(BF16)
    copies[1].wait()
    copies[2].wait()
    along = along_y(st[...].reshape(512, 256), y_both, y_high.astype(BF16))
    for copy in copies[5:]:
        copy.wait()
    partial = along_x(along, x_high, x_low)
    held = folded(jnp.concatenate([er[0], er[1]], axis=0), fold[...], rows[16:24], rows[24:32])
    row = lax.broadcasted_iota(jnp.int32, (8, LANES), 0)
    me = gx * n_z + gz
    keeper = jnp.where(row < 4, owner[0, 0], owner[0, 1])
    share = jnp.where(keeper == me, held, 0.0) - rows[0:8] * partial
    for c in range(CHUNKS):
        pay[c] = share[:, c * 128 : (c + 1) * 128]

    def prepare():
        rate = jnp.zeros((8, LANES), F32)
        limit = jnp.zeros((8, LANES), jnp.int32)
        for f in range(8):
            rate = jnp.where(row == f, relax[f // 4, f % 4], rate)
            limit = jnp.where(row == f, cutoff[f // 4, f % 4], limit)
        scale[...] = jnp.where(rows[8:16] <= (limit * limit).astype(F32), rate, 0.0)
        for part in range(2):
            tx_wide[part] = dot_0(pick[...], tx[part]).astype(BF16)
        by[...] = back_y_tables(y_high, y_low)

    n_far = 2 * (FAR[1] - FAR[0])
    n_near = 2 * n_z - 1 - n_far

    def remote(src, dst, which, target):
        return pltpu.make_async_remote_copy(
            src, dst, send_sem.at[which % 3], recv_sem.at[which], device_id=target, device_id_type=MESH
        )

    root = at(y, 16, 0)
    n_children = by_index({key: len(nodes) for key, nodes in children.items()}, 0)
    busy = [key for key, nodes in children.items() if key == (0, 1) or len(nodes) > 1]
    top = [(r, 0) for r in ROOTS]
    is_relay = jnp.logical_and(slot == 0, n_children == 1)

    def pass_on(key):
        for z, child_slot in children[key]:
            remote(total, total, 2, at(y, z, child_slot)).start()

    pl.semaphore_wait(barrier, n_children + jnp.where(is_root, len(ROOTS) + n_y - 2, len(ROOTS)))
    for r in ROOTS:
        from_root = (index + 2 * n_z - 2 * r) % (2 * n_z)
        far = jnp.logical_and(from_root >= 2 * FAR[0], from_root < 2 * FAR[1])
        after = jnp.where(from_root >= 2 * FAR[1], from_root - n_far, from_root) - 1
        place = jnp.where(far, n_near + from_root - 2 * FAR[0], after)

        @pl.when(index != 2 * r)
        def _():
            pltpu.make_async_remote_copy(
                pay, got.at[place], send_sem.at[0], recv_sem.at[jnp.where(far, 3, 0)],
                device_id=at(y, r, 0), device_id_type=MESH,
            ).start()

    prepare()

    @pl.when(jnp.logical_not(is_root))
    def _():
        remote(total, total, 2, root).wait_recv()

    @pl.when(is_root)
    def _():
        near, far = got.at[pl.ds(0, n_near)], got.at[pl.ds(n_near, n_far)]
        remote(near, near, 0, root).wait_recv()
        first = pay[...] + jnp.sum(near[...], axis=0)
        remote(far, far, 3, root).wait_recv()
        mine_y[...] = first + jnp.sum(far[...], axis=0)
        for step in sorted(range(1, n_y), key=lambda step: -min(step, n_y - step)):
            remote(mine_y, got_y.at[step - 1], 1, at((y + step) % n_y, gz, 0)).start()
        remote(got_y, got_y, 1, root).wait_recv()
        total[...] = mine_y[...] + jnp.sum(got_y[...], axis=0)

    for key in top + [key for key in busy if key not in top]:
        pl.when(index == 2 * key[0] + key[1])(functools.partial(pass_on, key))

    @pl.when(is_relay)
    def _():
        remote(total, total, 2, at(y, gz, 1)).start()

    summed = jnp.concatenate([total[c] for c in range(CHUNKS)], axis=1)
    added = back_y(back_x(summed * scale[...], tx_wide[...]), by[...])
    for h in range(2):
        block = added[256 * h : 256 * (h + 1)].reshape(4, 64, 256)
        out[h] = st[4 * h : 4 * h + 4] + block

    def pass_on_sent(count):
        sent = got.at[pl.ds(0, count)]
        remote(sent, sent, 2, root).wait_send()

    def shares_sent(count):
        sent = got.at[pl.ds(0, count)]
        remote(sent, sent, 0, root).wait_send()

    @pl.when(is_root)
    def _():
        remote(got_y, got_y, 1, root).wait_send()
        shares_sent(len(ROOTS) - 1)

    @pl.when(jnp.logical_not(is_root))
    def _():
        shares_sent(len(ROOTS))

    for key in busy:
        pl.when(index == 2 * key[0] + key[1])(functools.partial(pass_on_sent, len(children[key])))

    @pl.when(is_relay)
    def _():
        pass_on_sent(1)


def solution(mesh):
    n_gx, n_gy = mesh.shape["gx"], mesh.shape["gy"]
    tables = (along_y_tables(n_gy, FIELDS // 2), along_x_tables(n_gx), pick_table(), *fold_tables())

    def body(model_state, cutoff, relax_rate, owner_map, era_store):
        arrays = (cutoff, relax_rate, owner_map, model_state, era_store, *(jnp.asarray(t) for t in tables))
        vmem = pltpu.VMEM
        return pl.pallas_call(
            functools.partial(kernel, n_gx // 2, n_gy),
            out_shape=jax.ShapeDtypeStruct(model_state.shape, F32),
            in_specs=[pl.BlockSpec(memory_space=pltpu.HBM)] * 10,
            out_specs=pl.BlockSpec(memory_space=vmem),
            scratch_shapes=[
                pltpu.SMEM((2, 4), jnp.int32),
                pltpu.SMEM((2, 4), F32),
                pltpu.SMEM((1, 2), jnp.int32),
                vmem((8, 64, 256), F32),
                vmem((2, 4, 2 * NK * NK), F32),
                vmem((2, PAD, 256), BF16),
                vmem((2, WIDE, 256), BF16),
                vmem((WIDE, LANES), BF16),
                vmem((NK * NK, LANES), BF16),
                vmem((4 * FIELDS, LANES), F32),
                vmem((512, 512), BF16),
                vmem((2, LANES, 256), BF16),
                vmem((8, LANES), F32),
                vmem((CHUNKS, 8, 128), F32),
                vmem((2 * n_gy - 1, CHUNKS, 8, 128), F32),
                vmem((n_gx // 2 - 1, CHUNKS, 8, 128), F32),
                vmem((CHUNKS, 8, 128), F32),
                vmem((CHUNKS, 8, 128), F32),
                pltpu.SemaphoreType.DMA((11,)),
                pltpu.SemaphoreType.DMA((3,)),
                pltpu.SemaphoreType.DMA((4,)),
            ],
            compiler_params=pltpu.CompilerParams(
                collective_id=0, has_side_effects=True, vmem_limit_bytes=16 << 20
            ),
        )(*(pltpu.with_memory_space_constraint(array, pltpu.HBM) for array in arrays))

    placed = (
        P(None, "lev", "gy", "gx"),
        P(None, "lev"),
        P(None, "lev"),
        P("lev", None),
        P(("gx", "gy"), None, "lev", None),
    )
    return jax.shard_map(
        body, mesh=mesh, in_specs=placed, out_specs=P(None, "lev", "gy", "gx"), check_vma=False
    )
```
